32 devices in a mesh: lat: 8 (over z, y), lev: 4 (over x, core).
Axes of the slice: x: 2, y: 2, z: 4, core: 2. Of those that a mesh axis runs over, the one named last changes fastest.
Arguments:
- spec_in: bfloat16 [192, 171, 4, 512], P('lat', None, None, 'lev'), may hold values from -6 to 6
- cotangent: bfloat16 [192, 171, 4, 512], P('lat', None, None, 'lev'), may hold values from -6 to 6
- legendre: bfloat16 [192, 171, 256], P('lat'), may hold values from -0.4375 to 0.4375
- quad_weights: float32 [256], replicated, may hold values from 0.5 to 2
- wave_order: int32 [192], replicated, may hold values from 0 to 191, each once
- norm_gain: float32 [256], replicated, may hold values from 0.5 to 1.5
- weight_in: bfloat16 [256, 512], replicated, may hold values from -0.375 to 0.375
- bias_in: float32 [512], replicated, may hold values from -3 to 3
- weight_mid: bfloat16 [512, 512], replicated, may hold values from -0.25 to 0.25
- bias_mid: float32 [512], replicated, may hold values from -3 to 3
- weight_out: bfloat16 [512, 256], replicated, may hold values from -0.25 to 0.25
Outputs:
- grad_spec: float32 [192, 171, 4, 512], P('lat', None, None, 'lev')
- grad_gain: float32 [256], replicated
- grad_w_in: float32 [256, 512], replicated
- grad_b_in: float32 [512], replicated
- grad_w_mid: float32 [512, 512], replicated
- grad_b_mid: float32 [512], replicated
- grad_w_out: float32 [512, 256], replicated
The draws below stay inside these ranges and needn't reach their ends.
Inputs may be any that keep to these rules, and one draw needn't show every extreme that they name: `wave_order`: each of 0 to 191 appears once; a slot holding 171 or more is unused.
All inputs are finite; a program needn't handle non-finite values.
Results may differ from the reference program's by a relative error of at most 0.007.
Values may be sent and summed in bfloat16 or wider, within the bound.
No kernel may reach another device: no remote copies, remote signals or barrier semaphores. Data moves between devices by JAX's collectives and lax.ppermute only.
A program may use at most 256 MiB of HBM per device.

```python
import math
import jax
import jax.numpy as jnp
from jax import lax

WAVES = 171
SLOTS = 192
NLAT = 256
NLON = 512
HIDDEN_SIZE = 512
MEMBERS = 4
CHANNELS = 256
COLUMNS = 524288


def levels(stream_key, extent, cuts, least, high):
    level = 1.0
    for axis_at, shards_of in cuts:
        steps = jax.random.uniform(jax.random.fold_in(jax.random.fold_in(stream_key, 6), axis_at), (shards_of,), jnp.float32, least / len(cuts), high / len(cuts))
        level = level * jnp.repeat(jnp.exp(steps), extent[axis_at] // shards_of).reshape((-1,) + (1,) * (len(extent) - 1 - axis_at))
    return level


def noise(own_key, shape, spread, limit, split=(), kind=jnp.bfloat16):
    loudness = levels(own_key, shape, split, -0.22, 0.18) if split else 1.0
    drawn = jax.random.normal(own_key, shape, jnp.float32) * spread * loudness
    return jnp.minimum(jnp.maximum(drawn, -limit), limit).astype(kind)


def setup_inputs(seed: int = 0) -> dict:
    key_of = jax.random.split(jax.random.key(seed), 12)
    return {
        "spec_in": noise(key_of[0], (SLOTS, WAVES, MEMBERS, 2 * CHANNELS), 1.0, 6.0, ((0, 8), (3, 4))),
        "cotangent": noise(key_of[1], (SLOTS, WAVES, MEMBERS, 2 * CHANNELS), 1.0, 6.0, ((0, 8), (3, 4))),
        "legendre": noise(key_of[2], (SLOTS, WAVES, NLAT), WAVES ** -0.5, 0.4375, ((0, 8),)),
        "quad_weights": jnp.clip(jnp.exp(jax.random.uniform(key_of[3], (NLAT,), jnp.float32, math.log(0.5), math.log(2.0))), 0.5, 2.0),
        "wave_order": jax.random.permutation(key_of[4], SLOTS).astype(jnp.int32),
        "norm_gain": jnp.clip(1.0 + 0.1 * jax.random.normal(key_of[5], (CHANNELS,), jnp.float32), 0.5, 1.5),
        "weight_in": noise(key_of[6], (CHANNELS, HIDDEN_SIZE), CHANNELS ** -0.5, 0.375),
        "bias_in": noise(key_of[7], (HIDDEN_SIZE,), 0.5, 3.0, (), jnp.float32),
        "weight_mid": noise(key_of[8], (HIDDEN_SIZE, HIDDEN_SIZE), HIDDEN_SIZE ** -0.5, 0.25),
        "bias_mid": noise(key_of[9], (HIDDEN_SIZE,), 0.5, 3.0, (), jnp.float32),
        "weight_out": noise(key_of[10], (HIDDEN_SIZE, CHANNELS), HIDDEN_SIZE ** -0.5, 0.25),
    }


time_step = 0.5
norm_eps = 1e-06

def spectral_masks(waves_held, degree_count):
    degree = jnp.arange(degree_count, dtype=jnp.int32)
    living = (waves_held[:, None] <= degree[None, :]) & (waves_held[:, None] < WAVES)
    ratio = (degree * (degree + 1)).astype(jnp.float32) / float(WAVES * (WAVES - 1))
    factor = (1.0 / (1.0 + ratio * ratio)).astype(jnp.float32)
    shrink = jnp.where(living, factor[None, :], jnp.zeros_like(factor)[None, :])
    return (living, shrink)

def fourier_table(waves_all):
    longitude = jnp.arange(NLON, dtype=jnp.int32)
    phase_steps = waves_all[:, None] * longitude[None, :] % NLON
    angles = phase_steps.astype(jnp.float32) * (2.0 * math.pi / NLON)
    weight_scale = jnp.where(waves_all < WAVES, math.sqrt(2.0 / NLON), 0.0).astype(jnp.float32)[:, None]
    return jnp.stack([jnp.cos(angles) * weight_scale, -jnp.sin(angles) * weight_scale], axis=1).astype(jnp.bfloat16)

def contract_rows(left, right):
    return lax.dot_general(left, right, (((0,), (0,)), ((), ())), preferred_element_type=jnp.float32)

def contract_cols(left, right):
    return lax.dot_general(left, right, (((1,), (1,)), ((), ())), preferred_element_type=jnp.float32)

def column_grads(columns, column_cot, norm_gain, weight_in, bias_in, weight_mid, bias_mid, weight_out):
    inputs = columns.astype(jnp.float32)
    inverse = lax.rsqrt(lax.optimization_barrier(jnp.mean(inputs * inputs, axis=1, keepdims=True)) + norm_eps)
    gains = norm_gain.astype(jnp.float32)
    normed = (inputs * inverse * gains).astype(jnp.bfloat16)
    pre_one = jnp.dot(normed, weight_in, preferred_element_type=jnp.float32) + bias_in
    sig_one = jax.nn.sigmoid(pre_one)
    act_one = (pre_one * sig_one).astype(jnp.bfloat16)
    pre_two = jnp.dot(act_one, weight_mid, preferred_element_type=jnp.float32) + bias_mid
    sig_two = jax.nn.sigmoid(pre_two)
    act_two = (pre_two * sig_two).astype(jnp.bfloat16)
    gradient_third = contract_rows(act_two, column_cot)
    back_two = contract_cols(column_cot, weight_out)
    delta_two = (back_two * sig_two * (1.0 + pre_two * (1.0 - sig_two))).astype(jnp.bfloat16)
    gradient_second = contract_rows(act_one, delta_two)
    offset_second = lax.optimization_barrier(jnp.sum(delta_two.astype(jnp.float32), axis=0))
    back_one = contract_cols(delta_two, weight_mid)
    delta_one = (back_one * sig_one * (1.0 + pre_one * (1.0 - sig_one))).astype(jnp.bfloat16)
    gradient_first = contract_rows(normed, delta_one)
    offset_first = lax.optimization_barrier(jnp.sum(delta_one.astype(jnp.float32), axis=0))
    back_norm = contract_cols(delta_one, weight_in)
    gradient_gain = lax.optimization_barrier(jnp.sum(back_norm * inputs * inverse, axis=0))
    scaled = back_norm * gains
    grad_columns = inverse * scaled - inputs * inverse * inverse * inverse * lax.optimization_barrier(jnp.mean(scaled * inputs, axis=1, keepdims=True))
    return (grad_columns.astype(jnp.bfloat16), (gradient_gain, gradient_first, offset_first, gradient_second, offset_second, gradient_third))

def unpack_parts(packed):
    return jnp.transpose(packed.reshape(SLOTS, WAVES, MEMBERS, CHANNELS, 2), (0, 1, 2, 4, 3))

def reference(spec_in, cotangent, legendre, quad_weights, wave_order, norm_gain, weight_in, bias_in, weight_mid, bias_mid, weight_out):
    highest = lax.Precision.HIGHEST
    spec_in = unpack_parts(spec_in)
    cotangent = unpack_parts(cotangent)
    living, shrink = spectral_masks(wave_order, WAVES)
    basis_rows = jnp.where(living[:, :, None], legendre, jnp.zeros_like(legendre))
    wave_table = fourier_table(wave_order)
    basis_wide = basis_rows.astype(jnp.float32)
    table_wide = wave_table.astype(jnp.float32)
    fourier = jnp.einsum('slt,slepc->stepc', basis_wide, spec_in.astype(jnp.float32), precision=highest).astype(jnp.bfloat16)
    pushed = (time_step * cotangent.astype(jnp.float32) * shrink[:, :, None, None, None]).astype(jnp.bfloat16)
    pulled = jnp.einsum('slt,slepc->stepc', basis_wide, pushed.astype(jnp.float32), precision=highest)
    pulled = (quad_weights[None, :, None, None, None] * pulled).astype(jnp.bfloat16)
    grid_values = jnp.einsum('spo,stepc->otec', table_wide, fourier.astype(jnp.float32), precision=highest).astype(jnp.bfloat16)
    grid_cot = jnp.einsum('spo,stepc->otec', table_wide, pulled.astype(jnp.float32), precision=highest).astype(jnp.bfloat16)
    member_rows = jnp.transpose(grid_values, (2, 0, 1, 3)).reshape(MEMBERS, NLON * NLAT, CHANNELS)
    member_cots = jnp.transpose(grid_cot, (2, 0, 1, 3)).reshape(MEMBERS, NLON * NLAT, CHANNELS)

    def per_member(pair):
        return column_grads(pair[0], pair[1], norm_gain, weight_in, bias_in, weight_mid, bias_mid, weight_out)
    grad_rows, grads_all = lax.map(per_member, (member_rows, member_cots))
    factor = float(COLUMNS) ** (-0.5)
    grads = tuple((lax.optimization_barrier(jnp.sum(piece, axis=0)) * factor for piece in grads_all))
    grad_grid = jnp.transpose(grad_rows.reshape(MEMBERS, NLON, NLAT, CHANNELS), (1, 2, 0, 3))
    back_fourier = jnp.einsum('spo,otec->stepc', table_wide, grad_grid.astype(jnp.float32), precision=highest).astype(jnp.bfloat16)
    grad_spec = cotangent.astype(jnp.float32) * shrink[:, :, None, None, None] + jnp.einsum('slt,stepc->slepc', basis_wide, back_fourier.astype(jnp.float32), precision=highest)
    grad_spec = jnp.transpose(grad_spec, (0, 1, 2, 4, 3)).reshape(SLOTS, WAVES, MEMBERS, 2 * CHANNELS)
    return (grad_spec, grads[0], grads[1], grads[2], grads[3], grads[4], grads[5])
```

```python
import functools
import math

import jax
import jax.numpy as jnp
from jax import lax
from jax.experimental import pallas as pl
from jax.experimental.pallas import tpu as pltpu
from jax.sharding import PartitionSpec as P

WAVES = 171
TIME_STEP = 0.5
NORM_EPS = 1e-06
NLON = 512
F32 = jnp.float32
BF16 = jnp.bfloat16


def fourier_table(waves_all):
    longitude = jnp.arange(NLON, dtype=jnp.int32)
    phase_steps = waves_all[:, None] * longitude[None, :] % NLON
    angles = phase_steps.astype(F32) * (2.0 * math.pi / NLON)
    weight_scale = jnp.where(waves_all < WAVES, math.sqrt(2.0 / NLON), 0.0).astype(F32)[:, None]
    return jnp.concatenate(
        [jnp.cos(angles) * weight_scale, -jnp.sin(angles) * weight_scale], axis=0
    ).astype(BF16)


def shrink_factor(degree_count):
    degree = jnp.arange(degree_count, dtype=jnp.int32)
    ratio = (degree * (degree + 1)).astype(F32) / float(WAVES * (WAVES - 1))
    return (1.0 / (1.0 + ratio * ratio))[:, None]


def split_parts(half):
    width = 2 * half
    src = lax.broadcasted_iota(jnp.int32, (width, width), 0)
    dst = lax.broadcasted_iota(jnp.int32, (width, width), 1)
    group, inner = src // half, src % half
    target = (inner % 2) * half + group * (half // 2) + inner // 2
    return (target == dst).astype(BF16)


def dot(left, right):
    return jnp.dot(left, right, preferred_element_type=F32)


def dot_rows(left, right):
    return lax.dot_general(left, right, (((0,), (0,)), ((), ())), preferred_element_type=F32)


def legendre_kernel(pair, members, degrees, is_cot, waves, x_ref, leg_ref, *rest):
    if is_cot:
        factor_ref, quad_ref, out_ref, wide = rest
    else:
        out_ref, wide = rest
    step = pl.program_id(0)
    wide[...] = x_ref[...].astype(F32)
    lat_count, _, _, rows, lanes = out_ref.shape
    for k in range(pair):
        m = waves[step * pair + k]
        degree = lax.broadcasted_iota(jnp.int32, leg_ref.shape[1:], 0)
        living = (degree >= m) & (m < WAVES)
        basis = jnp.where(living, leg_ref[k].astype(F32), 0.0).astype(BF16)
        parts = []
        for e in range(members):
            part = wide[pl.ds(k * degrees * members + e, degrees, stride=members), :]
            if is_cot:
                part = TIME_STEP * part * factor_ref[...]
            parts.append(part.astype(BF16))
        result = dot_rows(basis, jnp.concatenate(parts, axis=1))
        if is_cot:
            result = result * quad_ref[...]
        result = result.astype(BF16)
        for e in range(members):
            out_ref[:, e, k] = result[:, e * lanes : (e + 1) * lanes].reshape(lat_count, rows, lanes)


def legendre(waves, packed, legendre_table, chunk, chunks, lat_count, factor=None, quad=None):
    slots, degrees, nlat = legendre_table.shape
    lanes = packed.shape[1]
    members = packed.shape[0] // (slots * degrees)
    pair = 4 if slots % 4 == 0 else 2
    span = nlat // chunks
    rows = span // lat_count
    is_cot = factor is not None
    block = pair * degrees * members
    in_specs = [
        pl.BlockSpec((block, lanes), lambda i, w: (i, 0)),
        pl.BlockSpec((pair, degrees, span), lambda i, w: (i, 0, chunk)),
    ]
    operands = [packed, legendre_table]
    if is_cot:
        in_specs += [
            pl.BlockSpec((degrees, 1), lambda i, w: (0, 0)),
            pl.BlockSpec((span, 1), lambda i, w: (chunk, 0)),
        ]
        operands += [factor, quad]
    return pl.pallas_call(
        functools.partial(legendre_kernel, pair, members, degrees, is_cot),
        out_shape=jax.ShapeDtypeStruct((lat_count, members, slots, rows, lanes), BF16),
        grid_spec=pltpu.PrefetchScalarGridSpec(
            num_scalar_prefetch=1,
            grid=(slots // pair,),
            in_specs=in_specs,
            out_specs=pl.BlockSpec(
                (lat_count, members, pair, rows, lanes), lambda i, w: (0, 0, i, 0, 0)
            ),
            scratch_shapes=[pltpu.VMEM((block, lanes), F32)],
        ),
        compiler_params=pltpu.CompilerParams(
            dimension_semantics=("arbitrary",), vmem_limit_bytes=60 << 20
        ),
        cost_estimate=pl.CostEstimate(
            flops=2 * slots * degrees * span * members * lanes,
            bytes_accessed=2 * packed.size + 2 * slots * span * (degrees + members * lanes),
            transcendentals=0,
        ),
        name="legendre_cot" if is_cot else "legendre_state",
    )(waves, *operands)


def inverse_kernel(pair, members, degrees, chunks, waves, cot_ref, leg_ref, factor_ref, *rest):
    backs = rest[:chunks]
    out_ref, wide = rest[chunks:]
    step = pl.program_id(0)
    wide[...] = cot_ref[...].astype(F32)
    lat_count, _, _, rows, lanes = backs[0].shape
    for k in range(pair):
        m = waves[step * pair + k]
        degree = lax.broadcasted_iota(jnp.int32, leg_ref.shape[1:], 0)
        basis = jnp.where((degree >= m) & (m < WAVES), leg_ref[k].astype(F32), 0.0).astype(BF16)
        column = lax.broadcasted_iota(jnp.int32, (degrees, 1), 0)
        shrink = jnp.where((column >= m) & (m < WAVES), factor_ref[...], 0.0)
        sides = []
        for e in range(members):
            sides.append(
                jnp.concatenate(
                    [b[:, e, k].reshape(lat_count * rows, lanes) for b in backs], axis=0
                )
            )
        result = dot(basis, jnp.concatenate(sides, axis=1))
        for e in range(members):
            where = pl.ds(k * degrees * members + e, degrees, stride=members)
            out_ref[where, :] = wide[where, :] * shrink + result[:, e * lanes : (e + 1) * lanes]


def inverse_legendre(waves, packed, legendre_table, factor, backs):
    slots, degrees, nlat = legendre_table.shape
    lanes = packed.shape[1]
    members = packed.shape[0] // (slots * degrees)
    pair = 4 if slots % 4 == 0 else 2
    block = pair * degrees * members
    lat_count, _, _, rows, _ = backs[0].shape
    chunks = len(backs)
    return pl.pallas_call(
        functools.partial(inverse_kernel, pair, members, degrees, chunks),
        out_shape=jax.ShapeDtypeStruct(packed.shape, F32),
        grid_spec=pltpu.PrefetchScalarGridSpec(
            num_scalar_prefetch=1,
            grid=(slots // pair,),
            in_specs=[
                pl.BlockSpec((block, lanes), lambda i, w: (i, 0)),
                pl.BlockSpec((pair, degrees, nlat), lambda i, w: (i, 0, 0)),
                pl.BlockSpec((degrees, 1), lambda i, w: (0, 0)),
            ]
            + [
                pl.BlockSpec((lat_count, members, pair, rows, lanes), lambda i, w: (0, 0, i, 0, 0))
            ]
            * chunks,
            out_specs=pl.BlockSpec((block, lanes), lambda i, w: (i, 0)),
            scratch_shapes=[pltpu.VMEM((block, lanes), F32)],
        ),
        compiler_params=pltpu.CompilerParams(
            dimension_semantics=("arbitrary",), vmem_limit_bytes=60 << 20
        ),
        cost_estimate=pl.CostEstimate(
            flops=2 * slots * degrees * nlat * members * lanes,
            bytes_accessed=6 * packed.size + 2 * slots * nlat * (degrees + members * lanes),
            transcendentals=0,
        ),
        name="inverse_legendre",
    )(waves, packed, legendre_table, factor, *backs)


def sigmoid(z):
    return 0.5 + 0.5 * jnp.tanh(0.5 * z)


def column_kernel(
    rows,
    block,
    state_ref,
    cot_ref,
    table_ref,
    back_table_ref,
    split_ref,
    merge_ref,
    gain_ref,
    w_in_ref,
    b_in_ref,
    w_mid_ref,
    b_mid_ref,
    w_in_t_ref,
    w_mid_t_ref,
    w_out_t_ref,
    out_ref,
    grad_ref,
    state_wide,
    cot_wide,
    out_wide,
    state_mat,
    cot_mat,
    back_acc,
):
    row, part = pl.program_id(0), pl.program_id(1)
    last_part = pl.num_programs(1) - 1
    lat_count, groups, slots_here, _, lanes = state_ref.shape
    slots = lat_count * slots_here
    hidden = w_in_ref.shape[1]
    channels = w_in_ref.shape[0]

    @pl.when((row == 0) & (part == 0))
    def _():
        grad_ref[...] = jnp.zeros_like(grad_ref)

        @pl.loop(0, lat_count)
        def _(i):
            size = slots_here * rows
            for j in range(groups):
                where = pl.ds(pl.multiple_of(i * size, 8), size)
                state_wide[j, where, :] = state_ref[i, j].astype(F32).reshape(size, lanes)
                cot_wide[j, where, :] = cot_ref[i, j].astype(F32).reshape(size, lanes)

    @pl.when(part == 0)
    def _():
        for wide, mat in ((state_wide, state_mat), (cot_wide, cot_mat)):
            for q in range(groups // 2):
                both = jnp.concatenate(
                    [wide[2 * q + j, pl.ds(row, slots, stride=rows), :].astype(BF16) for j in (0, 1)],
                    axis=1,
                )
                apart = dot(both, split_ref[...]).astype(BF16)
                for p in (0, 1):
                    mat[p * slots : (p + 1) * slots, q * lanes : (q + 1) * lanes] = apart[
                        :, p * lanes : (p + 1) * lanes
                    ]

    table = table_ref[pl.ds(pl.multiple_of(part * block, block), block), :]
    values = dot(table, state_mat[...]).astype(BF16).astype(F32)
    cot = dot(table, cot_mat[...]).astype(BF16)
    gain = gain_ref[...]
    inverse = lax.rsqrt(jnp.mean(values * values, axis=1, keepdims=True) + NORM_EPS)
    unit = values * inverse
    normed = (unit * gain).astype(BF16)
    pre_one = dot(normed, w_in_ref[...]) + b_in_ref[...]
    sig_one = sigmoid(pre_one)
    soft_one = pre_one * sig_one
    slope_one = sig_one + soft_one * (1.0 - sig_one)
    act_one = soft_one.astype(BF16)
    pre_two = dot(act_one, w_mid_ref[...]) + b_mid_ref[...]
    sig_two = sigmoid(pre_two)
    soft_two = pre_two * sig_two
    slope_two = sig_two + soft_two * (1.0 - sig_two)
    act_two = soft_two.astype(BF16)
    delta_two = (dot(cot, w_out_t_ref[...]) * slope_two).astype(BF16)
    delta_one = (dot(delta_two, w_mid_t_ref[...]) * slope_one).astype(BF16)
    back_norm = dot(delta_one, w_in_t_ref[...])
    grad_ref[:channels, :] += dot_rows(normed, delta_one)
    grad_ref[channels : channels + hidden, :] += dot_rows(act_one, delta_two)
    base = channels + hidden
    grad_ref[base : base + channels, :] += dot_rows(cot, act_two)
    base += channels
    grad_ref[base : base + 1, :] += jnp.sum(delta_one.astype(F32), axis=0, keepdims=True)
    grad_ref[base + 1 : base + 2, :] += jnp.sum(delta_two.astype(F32), axis=0, keepdims=True)
    grad_ref[base + 2 : base + 3, :channels] += jnp.sum(back_norm * unit, axis=0, keepdims=True)
    scaled = back_norm * gain
    mean = jnp.mean(scaled * values, axis=1, keepdims=True)
    grad_columns = (inverse * scaled - values * (inverse * inverse * inverse) * mean).astype(BF16)
    back = dot(back_table_ref[:, pl.ds(pl.multiple_of(part * block, block), block)], grad_columns)

    @pl.when(part == 0)
    def _():
        back_acc[...] = back

    @pl.when(part > 0)
    def _():
        back_acc[...] += back

    @pl.when(part == last_part)
    def _():
        for q in range(groups // 2):
            apart = jnp.concatenate(
                [
                    back_acc[p * slots : (p + 1) * slots, q * lanes : (q + 1) * lanes].astype(BF16)
                    for p in (0, 1)
                ],
                axis=1,
            )
            both = dot(apart, merge_ref[...])
            for j in (0, 1):
                out_wide[2 * q + j, pl.ds(row, slots, stride=rows), :] = both[
                    :, j * lanes : (j + 1) * lanes
                ]

    @pl.when((row == rows - 1) & (part == last_part))
    def _():
        @pl.loop(0, lat_count)
        def _(i):
            size = slots_here * rows
            for j in range(groups):
                where = pl.ds(pl.multiple_of(i * size, 8), size)
                out_ref[i, j] = out_wide[j, where, :].astype(BF16).reshape(slots_here, rows, lanes)


def column_grads(state, cot, table, back_table, split, merge, gain, weights):
    lat_count, groups, slots_here, rows, lanes = state.shape
    slots = lat_count * slots_here
    weight_in, bias_in, weight_mid, bias_mid, weight_out = weights
    channels, hidden = weight_in.shape
    block = NLON // 2
    grad_rows = 2 * channels + hidden + 8
    operands = [
        state,
        cot,
        table,
        back_table,
        split,
        merge,
        gain,
        weight_in,
        bias_in[None, :],
        weight_mid,
        bias_mid[None, :],
        weight_in.T,
        weight_mid.T,
        weight_out.T,
    ]

    def whole(shape):
        return pl.BlockSpec(shape, lambda i, j: (0,) * len(shape), pipeline_mode=pl.Buffered(1))

    out_shapes = (
        jax.ShapeDtypeStruct(state.shape, BF16),
        jax.ShapeDtypeStruct((grad_rows, hidden), F32),
    )
    wide = pltpu.VMEM((groups, slots * rows, lanes), F32)
    mat = pltpu.VMEM((2 * slots, channels), BF16)
    per_column = channels * hidden * 6 + hidden * hidden * 3 + 6 * slots * channels
    return pl.pallas_call(
        functools.partial(column_kernel, rows, block),
        out_shape=out_shapes,
        grid=(rows, NLON // block),
        in_specs=[whole(o.shape) for o in operands],
        out_specs=tuple(whole(o.shape) for o in out_shapes),
        scratch_shapes=[wide, wide, wide, mat, mat, pltpu.VMEM((2 * slots, channels), F32)],
        compiler_params=pltpu.CompilerParams(
            dimension_semantics=("arbitrary", "arbitrary"), vmem_limit_bytes=60 << 20
        ),
        cost_estimate=pl.CostEstimate(
            flops=2 * rows * NLON * per_column,
            bytes_accessed=6 * state.size + 4 * grad_rows * hidden,
            transcendentals=2 * rows * NLON * hidden,
        ),
        name="columns",
    )(*operands)


def local(
    spec_in,
    cotangent,
    legendre_table,
    quad_weights,
    wave_order,
    norm_gain,
    weight_in,
    bias_in,
    weight_mid,
    bias_mid,
    weight_out,
):
    axes = ("lat", "lev")
    slots_here, degrees, members, lanes = spec_in.shape
    nlat = legendre_table.shape[2]
    lat_count = lax.axis_size("lat")
    lev_count = lax.axis_size("lev")
    assert members == lev_count
    chunks = 2 if nlat // lat_count >= 16 else 1
    own_waves = lax.dynamic_slice_in_dim(wave_order, lax.axis_index("lat") * slots_here, slots_here)
    factor = shrink_factor(degrees)
    quad = quad_weights[:, None]
    spec_rows = spec_in.reshape(slots_here * degrees * members, lanes)
    cot_rows = cotangent.reshape(slots_here * degrees * members, lanes)
    count = lat_count * lev_count

    def exchange(x):
        shape = x.shape
        x = x.reshape((count,) + shape[2:])
        x = lax.all_to_all(x, axes, split_axis=0, concat_axis=0, tiled=True)
        return x.reshape(shape)

    table = fourier_table(wave_order)
    split = split_parts(lanes)
    received, before = [], None
    for k in range(chunks):
        state = legendre(own_waves, spec_rows, legendre_table, k, chunks, lat_count)
        if before is not None:
            state, before = lax.optimization_barrier((state, before))
            received[-1] = (received[-1][0], before)
        state = exchange(state)
        cot = legendre(own_waves, cot_rows, legendre_table, k, chunks, lat_count, factor, quad)
        cot, state = lax.optimization_barrier((cot, state))
        cot = before = exchange(cot)
        received.append((state, cot))
    weights = (weight_in, bias_in, weight_mid, bias_mid, weight_out)
    backs, totals = [], []
    for state, cot in received:
        back, grads = column_grads(
            state, cot, table.T, table, split, split.T, norm_gain[None, :], weights
        )
        backs.append(exchange(back))
        totals.append(grads)
    summed = lax.psum(functools.reduce(jnp.add, totals), axes)
    channels, hidden = weight_in.shape
    summed = summed * float(members * nlat * NLON) ** (-0.5)
    base = 2 * channels + hidden
    grad_w_in = summed[:channels]
    grad_w_mid = summed[channels : channels + hidden]
    grad_w_out = summed[channels + hidden : base].T
    grad_spec = inverse_legendre(own_waves, cot_rows, legendre_table, factor, backs)
    return (
        grad_spec.reshape(spec_in.shape),
        summed[base + 2, :channels],
        grad_w_in,
        summed[base],
        grad_w_mid,
        summed[base + 1],
        grad_w_out,
    )


def solution(mesh):
    placed = (
        P("lat", None, None, "lev"),
        P("lat", None, None, "lev"),
        P("lat", None, None),
    ) + (P(),) * 8
    return jax.shard_map(
        local,
        mesh=mesh,
        in_specs=placed,
        out_specs=(P("lat", None, None, "lev"),) + (P(),) * 6,
        check_vma=False,
    )
```

```python
import functools
import math

import jax
import jax.numpy as jnp
from jax import lax
from jax.experimental import pallas as pl
from jax.experimental.pallas import tpu as pltpu
from jax.sharding import PartitionSpec as P

WAVES = 171
TIME_STEP = 0.5
NORM_EPS = 1e-06
NLON = 512
F32 = jnp.float32
BF16 = jnp.bfloat16


def fourier_table(waves_all):
    longitude = jnp.arange(NLON, dtype=jnp.int32)
    phase_steps = waves_all[:, None] * longitude[None, :] % NLON
    angles = phase_steps.astype(F32) * (2.0 * math.pi / NLON)
    weight_scale = jnp.where(waves_all < WAVES, math.sqrt(2.0 / NLON), 0.0).astype(F32)[:, None]
    return jnp.concatenate(
        [jnp.cos(angles) * weight_scale, -jnp.sin(angles) * weight_scale], axis=0
    ).astype(BF16)


def shrink_factor(degree_count):
    degree = jnp.arange(degree_count, dtype=jnp.int32)
    ratio = (degree * (degree + 1)).astype(F32) / float(WAVES * (WAVES - 1))
    return (1.0 / (1.0 + ratio * ratio))[:, None]


def split_parts(half):
    width = 2 * half
    src = lax.broadcasted_iota(jnp.int32, (width, width), 0)
    dst = lax.broadcasted_iota(jnp.int32, (width, width), 1)
    group, inner = src // half, src % half
    target = (inner % 2) * half + group * (half // 2) + inner // 2
    return (target == dst).astype(BF16)


def dot(left, right):
    return jnp.dot(left, right, preferred_element_type=F32)


def dot_rows(left, right):
    return lax.dot_general(left, right, (((0,), (0,)), ((), ())), preferred_element_type=F32)


def legendre_kernel(pair, members, degrees, is_cot, waves, x_ref, leg_ref, *rest):
    if is_cot:
        factor_ref, quad_ref, out_ref, wide = rest
    else:
        out_ref, wide = rest
    step = pl.program_id(0)
    wide[...] = x_ref[...].astype(F32)
    lat_count, _, _, rows, lanes = out_ref.shape
    for k in range(pair):
        m = waves[step * pair + k]
        degree = lax.broadcasted_iota(jnp.int32, leg_ref.shape[1:], 0)
        living = (degree >= m) & (m < WAVES)
        basis = jnp.where(living, leg_ref[k].astype(F32), 0.0).astype(BF16)
        parts = []
        for e in range(members):
            part = wide[pl.ds(k * degrees * members + e, degrees, stride=members), :]
            if is_cot:
                part = TIME_STEP * part * factor_ref[...]
            parts.append(part.astype(BF16))
        result = dot_rows(basis, jnp.concatenate(parts, axis=1))
        if is_cot:
            result = result * quad_ref[...]
        result = result.astype(BF16)
        for e in range(members):
            out_ref[:, e, k] = result[:, e * lanes : (e + 1) * lanes].reshape(lat_count, rows, lanes)


def legendre(waves, packed, legendre_table, chunk, chunks, lat_count, factor=None, quad=None):
    slots, degrees, nlat = legendre_table.shape
    lanes = packed.shape[1]
    members = packed.shape[0] // (slots * degrees)
    pair = 4 if slots % 4 == 0 else 2
    span = nlat // chunks
    rows = span // lat_count
    is_cot = factor is not None
    block = pair * degrees * members
    in_specs = [
        pl.BlockSpec((block, lanes), lambda i, w: (i, 0)),
        pl.BlockSpec((pair, degrees, span), lambda i, w: (i, 0, chunk)),
    ]
    operands = [packed, legendre_table]
    if is_cot:
        in_specs += [
            pl.BlockSpec((degrees, 1), lambda i, w: (0, 0)),
            pl.BlockSpec((span, 1), lambda i, w: (chunk, 0)),
        ]
        operands += [factor, quad]
    return pl.pallas_call(
        functools.partial(legendre_kernel, pair, members, degrees, is_cot),
        out_shape=jax.ShapeDtypeStruct((lat_count, members, slots, rows, lanes), BF16),
        grid_spec=pltpu.PrefetchScalarGridSpec(
            num_scalar_prefetch=1,
            grid=(slots // pair,),
            in_specs=in_specs,
            out_specs=pl.BlockSpec(
                (lat_count, members, pair, rows, lanes), lambda i, w: (0, 0, i, 0, 0)
            ),
            scratch_shapes=[pltpu.VMEM((block, lanes), F32)],
        ),
        compiler_params=pltpu.CompilerParams(
            dimension_semantics=("arbitrary",), vmem_limit_bytes=60 << 20
        ),
        cost_estimate=pl.CostEstimate(
            flops=2 * slots * degrees * span * members * lanes,
            bytes_accessed=2 * packed.size + 2 * slots * span * (degrees + members * lanes),
            transcendentals=0,
        ),
        name="legendre_cot" if is_cot else "legendre_state",
    )(waves, *operands)


def inverse_kernel(pair, members, degrees, subs, waves, cot_ref, leg_ref, factor_ref, *rest):
    *backs, out_ref, wide = rest
    step = pl.program_id(0)
    wide[...] = cot_ref[...].astype(F32)
    lat_count, _, _, rows, lanes = backs[0].shape
    for k in range(pair):
        m = waves[step * pair + k]
        degree = lax.broadcasted_iota(jnp.int32, leg_ref.shape[1:], 0)
        basis = jnp.where((degree >= m) & (m < WAVES), leg_ref[k].astype(F32), 0.0).astype(BF16)
        column = lax.broadcasted_iota(jnp.int32, (degrees, 1), 0)
        shrink = jnp.where((column >= m) & (m < WAVES), factor_ref[...], 0.0)
        sides = []
        for e in range(members):
            pieces = []
            for first in range(0, len(backs), subs):
                subrows = [b[:, e, k].astype(F32) for b in backs[first : first + subs]]
                joined = jnp.concatenate(subrows, axis=1)
                pieces.append(joined.reshape(lat_count * subs * rows, lanes))
            sides.append(jnp.concatenate(pieces, axis=0).astype(BF16))
        result = dot(basis, jnp.concatenate(sides, axis=1))
        for e in range(members):
            where = pl.ds(k * degrees * members + e, degrees, stride=members)
            out_ref[where, :] = wide[where, :] * shrink + result[:, e * lanes : (e + 1) * lanes]


def inverse_legendre(waves, packed, legendre_table, factor, backs, subs):
    slots, degrees, nlat = legendre_table.shape
    lanes = packed.shape[1]
    members = packed.shape[0] // (slots * degrees)
    pair = 4 if slots % 4 == 0 else 2
    block = pair * degrees * members
    lat_count, _, _, rows, _ = backs[0].shape
    chunks = len(backs)
    return pl.pallas_call(
        functools.partial(inverse_kernel, pair, members, degrees, subs),
        out_shape=jax.ShapeDtypeStruct(packed.shape, F32),
        grid_spec=pltpu.PrefetchScalarGridSpec(
            num_scalar_prefetch=1,
            grid=(slots // pair,),
            in_specs=[
                pl.BlockSpec((block, lanes), lambda i, w: (i, 0)),
                pl.BlockSpec((pair, degrees, nlat), lambda i, w: (i, 0, 0)),
                pl.BlockSpec((degrees, 1), lambda i, w: (0, 0)),
            ]
            + [
                pl.BlockSpec((lat_count, members, pair, rows, lanes), lambda i, w: (0, 0, i, 0, 0))
            ]
            * chunks,
            out_specs=pl.BlockSpec((block, lanes), lambda i, w: (i, 0)),
            scratch_shapes=[pltpu.VMEM((block, lanes), F32)],
        ),
        compiler_params=pltpu.CompilerParams(
            dimension_semantics=("arbitrary",), vmem_limit_bytes=60 << 20
        ),
        cost_estimate=pl.CostEstimate(
            flops=2 * slots * degrees * nlat * members * lanes,
            bytes_accessed=6 * packed.size + 2 * slots * nlat * (degrees + members * lanes),
            transcendentals=0,
        ),
        name="inverse_legendre",
    )(waves, packed, legendre_table, factor, *backs)


def sigmoid(z):
    return 0.5 + 0.5 * jnp.tanh(0.5 * z)


def column_kernel(
    rows,
    block,
    chained,
    state_ref,
    cot_ref,
    table_ref,
    back_table_ref,
    split_ref,
    merge_ref,
    gain_ref,
    w_in_ref,
    b_in_ref,
    w_mid_ref,
    b_mid_ref,
    w_in_t_ref,
    w_mid_t_ref,
    w_out_t_ref,
    *rest,
):
    if chained:
        before_ref, *rest = rest
    out_ref, grad_ref, state_wide, cot_wide, out_wide, state_mat, cot_mat, back_acc = rest
    row, part = pl.program_id(0), pl.program_id(1)
    last_part = pl.num_programs(1) - 1
    lat_count, groups, slots_here, _, lanes = state_ref.shape
    slots = lat_count * slots_here
    hidden = w_in_ref.shape[1]
    channels = w_in_ref.shape[0]

    @pl.when((row == 0) & (part == 0))
    def _():
        grad_ref[...] = before_ref[...] if chained else jnp.zeros_like(grad_ref)

        @pl.loop(0, lat_count)
        def _(i):
            size = slots_here * rows
            for j in range(groups):
                where = pl.ds(pl.multiple_of(i * size, 8), size)
                state_wide[j, where, :] = state_ref[i, j].astype(F32).reshape(size, lanes)
                cot_wide[j, where, :] = cot_ref[i, j].astype(F32).reshape(size, lanes)

    @pl.when(part == 0)
    def _():
        for wide, mat in ((state_wide, state_mat), (cot_wide, cot_mat)):
            for q in range(groups // 2):
                both = jnp.concatenate(
                    [wide[2 * q + j, pl.ds(row, slots, stride=rows), :].astype(BF16) for j in (0, 1)],
                    axis=1,
                )
                apart = dot(both, split_ref[...]).astype(BF16)
                for p in (0, 1):
                    mat[p * slots : (p + 1) * slots, q * lanes : (q + 1) * lanes] = apart[
                        :, p * lanes : (p + 1) * lanes
                    ]

    table = table_ref[pl.ds(pl.multiple_of(part * block, block), block), :]
    values = dot(table, state_mat[...]).astype(BF16).astype(F32)
    cot = dot(table, cot_mat[...]).astype(BF16)
    gain = gain_ref[...]
    inverse = lax.rsqrt(jnp.mean(values * values, axis=1, keepdims=True) + NORM_EPS)
    unit = values * inverse
    normed = (unit * gain).astype(BF16)
    pre_one = dot(normed, w_in_ref[...]) + b_in_ref[...]
    sig_one = sigmoid(pre_one)
    soft_one = pre_one * sig_one
    slope_one = sig_one + soft_one * (1.0 - sig_one)
    act_one = soft_one.astype(BF16)
    pre_two = dot(act_one, w_mid_ref[...]) + b_mid_ref[...]
    sig_two = sigmoid(pre_two)
    soft_two = pre_two * sig_two
    slope_two = sig_two + soft_two * (1.0 - sig_two)
    act_two = soft_two.astype(BF16)
    delta_two = (dot(cot, w_out_t_ref[...]) * slope_two).astype(BF16)
    delta_one = (dot(delta_two, w_mid_t_ref[...]) * slope_one).astype(BF16)
    back_norm = dot(delta_one, w_in_t_ref[...])
    grad_ref[:channels, :] += dot_rows(normed, delta_one)
    grad_ref[channels : channels + hidden, :] += dot_rows(act_one, delta_two)
    base = channels + hidden
    grad_ref[base : base + channels, :] += dot_rows(cot, act_two)
    base += channels
    grad_ref[base : base + 1, :] += jnp.sum(delta_one.astype(F32), axis=0, keepdims=True)
    grad_ref[base + 1 : base + 2, :] += jnp.sum(delta_two.astype(F32), axis=0, keepdims=True)
    grad_ref[base + 2 : base + 3, :channels] += jnp.sum(back_norm * unit, axis=0, keepdims=True)
    scaled = back_norm * gain
    mean = jnp.mean(scaled * values, axis=1, keepdims=True)
    grad_columns = (inverse * scaled - values * (inverse * inverse * inverse) * mean).astype(BF16)
    back = dot(back_table_ref[:, pl.ds(pl.multiple_of(part * block, block), block)], grad_columns)

    @pl.when(part == 0)
    def _():
        back_acc[...] = back

    @pl.when(part > 0)
    def _():
        back_acc[...] += back

    @pl.when(part == last_part)
    def _():
        for q in range(groups // 2):
            apart = jnp.concatenate(
                [
                    back_acc[p * slots : (p + 1) * slots, q * lanes : (q + 1) * lanes].astype(BF16)
                    for p in (0, 1)
                ],
                axis=1,
            )
            both = dot(apart, merge_ref[...])
            for j in (0, 1):
                out_wide[2 * q + j, pl.ds(row, slots, stride=rows), :] = both[
                    :, j * lanes : (j + 1) * lanes
                ]

    @pl.when((row == rows - 1) & (part == last_part))
    def _():
        @pl.loop(0, lat_count)
        def _(i):
            size = slots_here * rows
            for j in range(groups):
                where = pl.ds(pl.multiple_of(i * size, 8), size)
                out_ref[i, j] = out_wide[j, where, :].astype(BF16).reshape(slots_here, rows, lanes)


def column_grads(state, cot, sub, rows, table, back_table, split, merge, gain, weights, before):
    lat_count, groups, slots_here, _, lanes = state.shape
    slots = lat_count * slots_here
    weight_in, bias_in, weight_mid, bias_mid, weight_out = weights
    channels, hidden = weight_in.shape
    block = NLON // 2
    grad_rows = -(-(2 * channels + hidden + 3) // 64) * 64
    operands = [
        table,
        back_table,
        split,
        merge,
        gain,
        weight_in,
        bias_in[None, :],
        weight_mid,
        bias_mid[None, :],
        weight_in.T,
        weight_mid.T,
        weight_out.T,
    ]
    if before is not None:
        operands.append(before)

    def whole(shape):
        return pl.BlockSpec(shape, lambda i, j: (0,) * len(shape), pipeline_mode=pl.Buffered(1))

    source = pl.BlockSpec(
        (lat_count, groups, slots_here, rows, lanes),
        lambda i, j: (0, 0, 0, sub, 0),
        pipeline_mode=pl.Buffered(1),
    )
    out_shapes = (
        jax.ShapeDtypeStruct((lat_count, groups, slots_here, rows, lanes), BF16),
        jax.ShapeDtypeStruct((grad_rows, hidden), F32),
    )
    wide = pltpu.VMEM((groups, slots * rows, lanes), F32)
    mat = pltpu.VMEM((2 * slots, channels), BF16)
    per_column = channels * hidden * 6 + hidden * hidden * 3 + 6 * slots * channels
    return pl.pallas_call(
        functools.partial(column_kernel, rows, block, before is not None),
        out_shape=out_shapes,
        grid=(rows, NLON // block),
        in_specs=[source, source] + [whole(o.shape) for o in operands],
        out_specs=tuple(whole(o.shape) for o in out_shapes),
        scratch_shapes=[wide, wide, wide, mat, mat, pltpu.VMEM((2 * slots, channels), F32)],
        compiler_params=pltpu.CompilerParams(
            dimension_semantics=("arbitrary", "arbitrary"), vmem_limit_bytes=60 << 20
        ),
        cost_estimate=pl.CostEstimate(
            flops=2 * rows * NLON * per_column,
            bytes_accessed=6 * slots * rows * groups * lanes + 8 * grad_rows * hidden,
            transcendentals=2 * rows * NLON * hidden,
        ),
        name="columns",
    )(state, cot, *operands)


def swap(x, axis, bits):
    return lax.ppermute(x, axis, [(i, i ^ bits) for i in range(lax.axis_size(axis))])


def reduce_grads(total):
    top = lax.axis_size("lat") // 4
    steps = []
    for axis, limit in (("lev", lax.axis_size("lev")), ("lat", top)):
        bit = 1
        while bit < limit:
            steps.append((axis, bit))
            bit *= 2
    for axis, bit in steps:
        size = total.shape[0] // 2
        side = (lax.axis_index(axis) // bit) % 2
        sent = lax.dynamic_slice_in_dim(total, (1 - side) * size, size).astype(BF16)
        kept = lax.dynamic_slice_in_dim(total, side * size, size)
        total = kept + swap(sent, axis, bit).astype(F32)
    part = total.astype(BF16)
    one, two, three = (swap(part, "lat", k * top).astype(F32) for k in (1, 2, 3))
    part = ((part.astype(F32) + one) + (two + three)).astype(BF16)
    for axis, bit in reversed(steps):
        side = (lax.axis_index(axis) // bit) % 2
        other = swap(part, axis, bit)
        first, second = jnp.where(side == 0, part, other), jnp.where(side == 0, other, part)
        part = jnp.concatenate([first, second], axis=0)
    return part.astype(F32)


def step(
    spec_in,
    cotangent,
    legendre_table,
    quad_weights,
    wave_order,
    norm_gain,
    weight_in,
    bias_in,
    weight_mid,
    bias_mid,
    weight_out,
):
    axes = ("lat", "lev")
    slots_here, degrees, members, lanes = spec_in.shape
    nlat = legendre_table.shape[2]
    lat_count = lax.axis_size("lat")
    lev_count = lax.axis_size("lev")
    assert members == lev_count
    chunks = 2 if nlat // lat_count >= 16 else 1
    own_waves = lax.dynamic_slice_in_dim(wave_order, lax.axis_index("lat") * slots_here, slots_here)
    factor = shrink_factor(degrees)
    quad = quad_weights[:, None]
    spec_rows = spec_in.reshape(slots_here * degrees * members, lanes)
    cot_rows = cotangent.reshape(slots_here * degrees * members, lanes)
    count = lat_count * lev_count

    def exchange(x):
        shape = x.shape
        x = x.reshape((count,) + shape[2:])
        x = lax.all_to_all(x, axes, split_axis=0, concat_axis=0, tiled=True)
        return x.reshape(shape)

    table = fourier_table(wave_order)
    split = split_parts(lanes)
    rows = nlat // chunks // lat_count
    subs = rows // 8
    received, before = [], None
    for k in range(chunks):
        state = legendre(own_waves, spec_rows, legendre_table, k, chunks, lat_count)
        if before is not None:
            state, before = lax.optimization_barrier((state, before))
            received[-1] = (received[-1][0], before)
        state = exchange(state)
        cot = legendre(own_waves, cot_rows, legendre_table, k, chunks, lat_count, factor, quad)
        cot, state = lax.optimization_barrier((cot, state))
        cot = before = exchange(cot)
        received.append((state, cot))
    weights = (weight_in, bias_in, weight_mid, bias_mid, weight_out)
    gain = norm_gain[None, :]
    backs, total = [], None
    for state, cot in received:
        for sub in range(subs):
            back, total = column_grads(
                state, cot, sub, rows // subs, table.T, table, split, split.T, gain, weights, total
            )
            backs.append(exchange(back))
    summed = reduce_grads(total)
    channels, hidden = weight_in.shape
    summed = summed * float(members * nlat * NLON) ** (-0.5)
    base = 2 * channels + hidden
    grad_w_in = summed[:channels]
    grad_w_mid = summed[channels : channels + hidden]
    grad_w_out = summed[channels + hidden : base].T
    grad_spec = inverse_legendre(own_waves, cot_rows, legendre_table, factor, backs, subs)
    return (
        grad_spec.reshape(spec_in.shape),
        summed[base + 2, :channels],
        grad_w_in,
        summed[base],
        grad_w_mid,
        summed[base + 1],
        grad_w_out,
    )


def solution(mesh):
    placed = (
        P("lat", None, None, "lev"),
        P("lat", None, None, "lev"),
        P("lat", None, None),
    ) + (P(),) * 8
    return jax.shard_map(
        step,
        mesh=mesh,
        in_specs=placed,
        out_specs=(P("lat", None, None, "lev"),) + (P(),) * 6,
        check_vma=False,
    )
```

```python
import functools
import math

import jax
import jax.numpy as jnp
from jax import lax
from jax.experimental import pallas as pl
from jax.experimental.pallas import tpu as pltpu
from jax.sharding import PartitionSpec as P

WAVES = 171
TIME_STEP = 0.5
NORM_EPS = 1e-06
NLON = 512
F32 = jnp.float32
BF16 = jnp.bfloat16


def fourier_table(waves_all):
    longitude = jnp.arange(NLON, dtype=jnp.int32)
    phase_steps = waves_all[:, None] * longitude[None, :] % NLON
    angles = phase_steps.astype(F32) * (2.0 * math.pi / NLON)
    weight_scale = jnp.where(waves_all < WAVES, math.sqrt(2.0 / NLON), 0.0).astype(F32)[:, None]
    return jnp.concatenate(
        [jnp.cos(angles) * weight_scale, -jnp.sin(angles) * weight_scale], axis=0
    ).astype(BF16)


def shrink_factor(degree_count):
    degree = jnp.arange(degree_count, dtype=jnp.int32)
    ratio = (degree * (degree + 1)).astype(F32) / float(WAVES * (WAVES - 1))
    return (1.0 / (1.0 + ratio * ratio))[:, None]


def split_parts(half):
    width = 2 * half
    src = lax.broadcasted_iota(jnp.int32, (width, width), 0)
    dst = lax.broadcasted_iota(jnp.int32, (width, width), 1)
    group, inner = src // half, src % half
    target = (inner % 2) * half + group * (half // 2) + inner // 2
    return (target == dst).astype(BF16)


def dot(left, right):
    return jnp.dot(left, right, preferred_element_type=F32)


def dot_rows(left, right):
    return lax.dot_general(left, right, (((0,), (0,)), ((), ())), preferred_element_type=F32)


def legendre_kernel(
    pair, members, degrees, waves, x_ref, y_ref, leg_ref, factor_ref, quad_ref, out_ref, x_wide, y_wide
):
    step = pl.program_id(0)
    x_wide[...] = x_ref[...].astype(F32)
    y_wide[...] = y_ref[...].astype(F32)
    lat_count, _, _, _, rows, lanes = out_ref.shape
    for k in range(pair):
        m = waves[step * pair + k]
        degree = lax.broadcasted_iota(jnp.int32, leg_ref.shape[1:], 0)
        living = (degree >= m) & (m < WAVES)
        basis = jnp.where(living, leg_ref[k].astype(F32), 0.0).astype(BF16)
        for is_cot, wide in enumerate((x_wide, y_wide)):
            parts = []
            for e in range(members):
                part = wide[pl.ds(k * degrees * members + e, degrees, stride=members), :]
                if is_cot:
                    part = TIME_STEP * part * factor_ref[...]
                parts.append(part.astype(BF16))
            result = dot_rows(basis, jnp.concatenate(parts, axis=1))
            if is_cot:
                result = result * quad_ref[...]
            result = result.astype(BF16)
            for e in range(members):
                out_ref[:, e, is_cot, k] = result[:, e * lanes : (e + 1) * lanes].reshape(
                    lat_count, rows, lanes
                )


def legendre(waves, spec, cot, legendre_table, chunk, chunks, lat_count, factor, quad):
    slots, degrees, nlat = legendre_table.shape
    lanes = spec.shape[1]
    members = spec.shape[0] // (slots * degrees)
    pair = 4 if slots % 4 == 0 else 2
    span = nlat // chunks
    rows = span // lat_count
    block = pair * degrees * members
    packed = pl.BlockSpec((block, lanes), lambda i, w: (i, 0))
    return pl.pallas_call(
        functools.partial(legendre_kernel, pair, members, degrees),
        out_shape=jax.ShapeDtypeStruct((lat_count, members, 2, slots, rows, lanes), BF16),
        grid_spec=pltpu.PrefetchScalarGridSpec(
            num_scalar_prefetch=1,
            grid=(slots // pair,),
            in_specs=[
                packed,
                packed,
                pl.BlockSpec((pair, degrees, span), lambda i, w: (i, 0, chunk)),
                pl.BlockSpec((degrees, 1), lambda i, w: (0, 0)),
                pl.BlockSpec((span, 1), lambda i, w: (chunk, 0)),
            ],
            out_specs=pl.BlockSpec(
                (lat_count, members, 2, pair, rows, lanes), lambda i, w: (0, 0, 0, i, 0, 0)
            ),
            scratch_shapes=[pltpu.VMEM((block, lanes), F32)] * 2,
        ),
        compiler_params=pltpu.CompilerParams(
            dimension_semantics=("arbitrary",), vmem_limit_bytes=60 << 20
        ),
        cost_estimate=pl.CostEstimate(
            flops=4 * slots * degrees * span * members * lanes,
            bytes_accessed=4 * spec.size + 2 * slots * span * (degrees + 2 * members * lanes),
            transcendentals=0,
        ),
        name="legendre",
    )(waves, spec, cot, legendre_table, factor, quad)


def inverse_kernel(pair, members, degrees, counts, waves, cot_ref, leg_ref, factor_ref, *rest):
    *backs, out_ref, wide = rest
    step = pl.program_id(0)
    wide[...] = cot_ref[...].astype(F32)
    lanes = cot_ref.shape[1]
    for k in range(pair):
        m = waves[step * pair + k]
        degree = lax.broadcasted_iota(jnp.int32, leg_ref.shape[1:], 0)
        basis = jnp.where((degree >= m) & (m < WAVES), leg_ref[k].astype(F32), 0.0).astype(BF16)
        column = lax.broadcasted_iota(jnp.int32, (degrees, 1), 0)
        shrink = jnp.where((column >= m) & (m < WAVES), factor_ref[...], 0.0)
        sides = []
        for e in range(members):
            pieces, rest_backs = [], list(backs)
            for subs in counts:
                joined = [rest_backs.pop(0)[:, e, k].astype(F32) for _ in range(subs)]
                joined = jnp.concatenate(joined, axis=1) if subs > 1 else joined[0]
                pieces.append(joined.reshape(-1, lanes))
            sides.append(jnp.concatenate(pieces, axis=0).astype(BF16))
        result = dot(basis, jnp.concatenate(sides, axis=1))
        for e in range(members):
            where = pl.ds(k * degrees * members + e, degrees, stride=members)
            out_ref[where, :] = wide[where, :] * shrink + result[:, e * lanes : (e + 1) * lanes]


def inverse_legendre(waves, packed, legendre_table, factor, backs, counts):
    slots, degrees, nlat = legendre_table.shape
    lanes = packed.shape[1]
    members = packed.shape[0] // (slots * degrees)
    pair = 4 if slots % 4 == 0 else 2
    block = pair * degrees * members
    return pl.pallas_call(
        functools.partial(inverse_kernel, pair, members, degrees, counts),
        out_shape=jax.ShapeDtypeStruct(packed.shape, F32),
        grid_spec=pltpu.PrefetchScalarGridSpec(
            num_scalar_prefetch=1,
            grid=(slots // pair,),
            in_specs=[
                pl.BlockSpec((block, lanes), lambda i, w: (i, 0)),
                pl.BlockSpec((pair, degrees, nlat), lambda i, w: (i, 0, 0)),
                pl.BlockSpec((degrees, 1), lambda i, w: (0, 0)),
            ]
            + [
                pl.BlockSpec(b.shape[:2] + (pair,) + b.shape[3:], lambda i, w: (0, 0, i, 0, 0))
                for b in backs
            ],
            out_specs=pl.BlockSpec((block, lanes), lambda i, w: (i, 0)),
            scratch_shapes=[pltpu.VMEM((block, lanes), F32)],
        ),
        compiler_params=pltpu.CompilerParams(
            dimension_semantics=("arbitrary",), vmem_limit_bytes=60 << 20
        ),
        cost_estimate=pl.CostEstimate(
            flops=2 * slots * degrees * nlat * members * lanes,
            bytes_accessed=6 * packed.size + 2 * slots * nlat * (degrees + members * lanes),
            transcendentals=0,
        ),
        name="inverse_legendre",
    )(waves, packed, legendre_table, factor, *backs)


def sigmoid(z):
    return 0.5 + 0.5 * jnp.tanh(0.5 * z)


def column_kernel(
    rows,
    block,
    chained,
    state_ref,
    cot_ref,
    table_ref,
    back_table_ref,
    split_ref,
    merge_ref,
    gain_ref,
    w_in_ref,
    b_in_ref,
    w_mid_ref,
    b_mid_ref,
    w_in_t_ref,
    w_mid_t_ref,
    w_out_t_ref,
    *rest,
):
    if chained:
        before_ref, *rest = rest
    out_ref, grad_ref, state_wide, cot_wide, out_wide, state_mat, cot_mat, back_acc = rest
    row, part = pl.program_id(0), pl.program_id(1)
    last_part = pl.num_programs(1) - 1
    lat_count, groups, slots_here, _, lanes = state_ref.shape
    slots = lat_count * slots_here
    hidden = w_in_ref.shape[1]
    channels = w_in_ref.shape[0]

    @pl.when((row == 0) & (part == 0))
    def _():
        grad_ref[...] = before_ref[...] if chained else jnp.zeros_like(grad_ref)

        @pl.loop(0, lat_count)
        def _(i):
            size = slots_here * rows
            for j in range(groups):
                where = pl.ds(pl.multiple_of(i * size, 8), size)
                state_wide[j, where, :] = state_ref[i, j].astype(F32).reshape(size, lanes)
                cot_wide[j, where, :] = cot_ref[i, j].astype(F32).reshape(size, lanes)

    @pl.when(part == 0)
    def _():
        for wide, mat in ((state_wide, state_mat), (cot_wide, cot_mat)):
            for q in range(groups // 2):
                both = jnp.concatenate(
                    [wide[2 * q + j, pl.ds(row, slots, stride=rows), :].astype(BF16) for j in (0, 1)],
                    axis=1,
                )
                apart = dot(both, split_ref[...]).astype(BF16)
                for p in (0, 1):
                    mat[p * slots : (p + 1) * slots, q * lanes : (q + 1) * lanes] = apart[
                        :, p * lanes : (p + 1) * lanes
                    ]

    table = table_ref[pl.ds(pl.multiple_of(part * block, block), block), :]
    values = dot(table, state_mat[...]).astype(BF16).astype(F32)
    cot = dot(table, cot_mat[...]).astype(BF16)
    gain = gain_ref[...]
    inverse = lax.rsqrt(jnp.mean(values * values, axis=1, keepdims=True) + NORM_EPS)
    unit = values * inverse
    normed = (unit * gain).astype(BF16)
    pre_one = dot(normed, w_in_ref[...]) + b_in_ref[...]
    sig_one = sigmoid(pre_one)
    soft_one = pre_one * sig_one
    slope_one = sig_one + soft_one * (1.0 - sig_one)
    act_one = soft_one.astype(BF16)
    pre_two = dot(act_one, w_mid_ref[...]) + b_mid_ref[...]
    sig_two = sigmoid(pre_two)
    soft_two = pre_two * sig_two
    slope_two = sig_two + soft_two * (1.0 - sig_two)
    act_two = soft_two.astype(BF16)
    delta_two = (dot(cot, w_out_t_ref[...]) * slope_two).astype(BF16)
    delta_one = (dot(delta_two, w_mid_t_ref[...]) * slope_one).astype(BF16)
    back_norm = dot(delta_one, w_in_t_ref[...])
    grad_ref[:channels, :] += dot_rows(normed, delta_one)
    grad_ref[channels : channels + hidden, :] += dot_rows(act_one, delta_two)
    base = channels + hidden
    grad_ref[base : base + channels, :] += dot_rows(cot, act_two)
    base += channels
    grad_ref[base : base + 1, :] += jnp.sum(delta_one.astype(F32), axis=0, keepdims=True)
    grad_ref[base + 1 : base + 2, :] += jnp.sum(delta_two.astype(F32), axis=0, keepdims=True)
    grad_ref[base + 2 : base + 3, :channels] += jnp.sum(back_norm * unit, axis=0, keepdims=True)
    scaled = back_norm * gain
    mean = jnp.mean(scaled * values, axis=1, keepdims=True)
    grad_columns = (inverse * scaled - values * (inverse * inverse * inverse) * mean).astype(BF16)
    back = dot(back_table_ref[:, pl.ds(pl.multiple_of(part * block, block), block)], grad_columns)

    @pl.when(part == 0)
    def _():
        back_acc[...] = back

    @pl.when(part > 0)
    def _():
        back_acc[...] += back

    @pl.when(part == last_part)
    def _():
        for q in range(groups // 2):
            apart = jnp.concatenate(
                [
                    back_acc[p * slots : (p + 1) * slots, q * lanes : (q + 1) * lanes].astype(BF16)
                    for p in (0, 1)
                ],
                axis=1,
            )
            both = dot(apart, merge_ref[...])
            for j in (0, 1):
                out_wide[2 * q + j, pl.ds(row, slots, stride=rows), :] = both[
                    :, j * lanes : (j + 1) * lanes
                ]

    @pl.when((row == rows - 1) & (part == last_part))
    def _():
        @pl.loop(0, lat_count)
        def _(i):
            size = slots_here * rows
            for j in range(groups):
                where = pl.ds(pl.multiple_of(i * size, 8), size)
                out_ref[i, j] = out_wide[j, where, :].astype(BF16).reshape(slots_here, rows, lanes)


def column_grads(pair, sub, rows, table, back_table, split, merge, gain, weights, before):
    lat_count, groups, _, slots_here, _, lanes = pair.shape
    slots = lat_count * slots_here
    weight_in, bias_in, weight_mid, bias_mid, weight_out = weights
    channels, hidden = weight_in.shape
    block = NLON // 2
    grad_rows = -(-(2 * channels + hidden + 3) // 64) * 64
    operands = [
        table,
        back_table,
        split,
        merge,
        gain,
        weight_in,
        bias_in[None, :],
        weight_mid,
        bias_mid[None, :],
        weight_in.T,
        weight_mid.T,
        weight_out.T,
    ]
    if before is not None:
        operands.append(before)

    def whole(shape):
        return pl.BlockSpec(shape, lambda i, j: (0,) * len(shape), pipeline_mode=pl.Buffered(1))

    def source(which):
        return pl.BlockSpec(
            (lat_count, groups, None, slots_here, rows, lanes),
            lambda i, j: (0, 0, which, 0, sub, 0),
            pipeline_mode=pl.Buffered(1),
        )

    out_shapes = (
        jax.ShapeDtypeStruct((lat_count, groups, slots_here, rows, lanes), BF16),
        jax.ShapeDtypeStruct((grad_rows, hidden), F32),
    )
    wide = pltpu.VMEM((groups, slots * rows, lanes), F32)
    mat = pltpu.VMEM((2 * slots, channels), BF16)
    per_column = channels * hidden * 6 + hidden * hidden * 3 + 6 * slots * channels
    return pl.pallas_call(
        functools.partial(column_kernel, rows, block, before is not None),
        out_shape=out_shapes,
        grid=(rows, NLON // block),
        in_specs=[source(0), source(1)] + [whole(o.shape) for o in operands],
        out_specs=tuple(whole(o.shape) for o in out_shapes),
        scratch_shapes=[wide, wide, wide, mat, mat, pltpu.VMEM((2 * slots, channels), F32)],
        compiler_params=pltpu.CompilerParams(
            dimension_semantics=("arbitrary", "arbitrary"), vmem_limit_bytes=60 << 20
        ),
        cost_estimate=pl.CostEstimate(
            flops=2 * rows * NLON * per_column,
            bytes_accessed=6 * slots * rows * groups * lanes + 8 * grad_rows * hidden,
            transcendentals=2 * rows * NLON * hidden,
        ),
        name="columns",
    )(pair, pair, *operands)


def swap(x, axis, bits):
    return lax.ppermute(x, axis, [(i, i ^ bits) for i in range(lax.axis_size(axis))])


def reduce_grads(total):
    top = lax.axis_size("lat") // 4
    steps = []
    for axis, limit in (("lev", lax.axis_size("lev")), ("lat", top)):
        bit = 1
        while bit < limit:
            steps.append((axis, bit))
            bit *= 2
    for axis, bit in steps:
        size = total.shape[0] // 2
        side = (lax.axis_index(axis) // bit) % 2
        sent = lax.dynamic_slice_in_dim(total, (1 - side) * size, size).astype(BF16)
        kept = lax.dynamic_slice_in_dim(total, side * size, size)
        total = kept + swap(sent, axis, bit).astype(F32)
    part = total.astype(BF16)
    one, two, three = (swap(part, "lat", k * top).astype(F32) for k in (1, 2, 3))
    part = ((part.astype(F32) + one) + (two + three)).astype(BF16)
    for axis, bit in reversed(steps):
        side = (lax.axis_index(axis) // bit) % 2
        other = swap(part, axis, bit)
        first, second = jnp.where(side == 0, part, other), jnp.where(side == 0, other, part)
        part = jnp.concatenate([first, second], axis=0)
    return part.astype(F32)


def step(
    spec_in,
    cotangent,
    legendre_table,
    quad_weights,
    wave_order,
    norm_gain,
    weight_in,
    bias_in,
    weight_mid,
    bias_mid,
    weight_out,
):
    axes = ("lat", "lev")
    slots_here, degrees, members, lanes = spec_in.shape
    nlat = legendre_table.shape[2]
    lat_count = lax.axis_size("lat")
    lev_count = lax.axis_size("lev")
    assert members == lev_count
    chunks = 2 if nlat // lat_count >= 16 else 1
    own_waves = lax.dynamic_slice_in_dim(wave_order, lax.axis_index("lat") * slots_here, slots_here)
    factor = shrink_factor(degrees)
    quad = quad_weights[:, None]
    spec_rows = spec_in.reshape(slots_here * degrees * members, lanes)
    cot_rows = cotangent.reshape(slots_here * degrees * members, lanes)
    count = lat_count * lev_count

    def exchange(x):
        shape = x.shape
        x = x.reshape((count,) + shape[2:])
        x = lax.all_to_all(x, axes, split_axis=0, concat_axis=0, tiled=True)
        return x.reshape(shape)

    table = fourier_table(wave_order)
    split = split_parts(lanes)
    rows = nlat // chunks // lat_count
    subs = rows // 8
    received = []
    for k in range(chunks):
        pair = legendre(
            own_waves, spec_rows, cot_rows, legendre_table, k, chunks, lat_count, factor, quad
        )
        if received:
            pair, received[-1] = lax.optimization_barrier((pair, received[-1]))
        received.append(exchange(pair))
    weights = (weight_in, bias_in, weight_mid, bias_mid, weight_out)
    gain = norm_gain[None, :]
    counts = (1,) * (chunks - 1) + (subs,)
    backs, total = [], None
    for k, pair in enumerate(received):
        for sub in range(counts[k]):
            back, total = column_grads(
                pair, sub, rows // counts[k], table.T, table, split, split.T, gain, weights, total
            )
            backs.append(exchange(back))
    summed = reduce_grads(total)
    channels, hidden = weight_in.shape
    summed = summed * float(members * nlat * NLON) ** (-0.5)
    base = 2 * channels + hidden
    grad_w_in = summed[:channels]
    grad_w_mid = summed[channels : channels + hidden]
    grad_w_out = summed[channels + hidden : base].T
    grad_spec = inverse_legendre(own_waves, cot_rows, legendre_table, factor, backs, counts)
    return (
        grad_spec.reshape(spec_in.shape),
        summed[base + 2, :channels],
        grad_w_in,
        summed[base],
        grad_w_mid,
        summed[base + 1],
        grad_w_out,
    )


def solution(mesh):
    placed = (
        P("lat", None, None, "lev"),
        P("lat", None, None, "lev"),
        P("lat", None, None),
    ) + (P(),) * 8
    return jax.shard_map(
        step,
        mesh=mesh,
        in_specs=placed,
        out_specs=(P("lat", None, None, "lev"),) + (P(),) * 6,
        check_vma=False,
    )
```

```python
import functools
import math

import jax
import jax.numpy as jnp
from jax import lax
from jax.experimental import pallas as pl
from jax.experimental.pallas import tpu as pltpu
from jax.sharding import PartitionSpec as P

WAVES = 171
TIME_STEP = 0.5
NORM_EPS = 1e-06
NLON = 512
F32 = jnp.float32
BF16 = jnp.bfloat16


def fourier_table(waves_all):
    longitude = jnp.arange(NLON, dtype=jnp.int32)
    phase_steps = waves_all[:, None] * longitude[None, :] % NLON
    angles = phase_steps.astype(F32) * (2.0 * math.pi / NLON)
    weight_scale = jnp.where(waves_all < WAVES, math.sqrt(2.0 / NLON), 0.0).astype(F32)[:, None]
    return jnp.concatenate(
        [jnp.cos(angles) * weight_scale, -jnp.sin(angles) * weight_scale], axis=0
    ).astype(BF16)


def shrink_factor(degree_count):
    degree = jnp.arange(degree_count, dtype=jnp.int32)
    ratio = (degree * (degree + 1)).astype(F32) / float(WAVES * (WAVES - 1))
    return (1.0 / (1.0 + ratio * ratio))[:, None]


def split_parts(half):
    width = 2 * half
    src = lax.broadcasted_iota(jnp.int32, (width, width), 0)
    dst = lax.broadcasted_iota(jnp.int32, (width, width), 1)
    group, inner = src // half, src % half
    target = (inner % 2) * half + group * (half // 2) + inner // 2
    return (target == dst).astype(BF16)


def dot(left, right):
    return jnp.dot(left, right, preferred_element_type=F32)


def dot_rows(left, right):
    return lax.dot_general(left, right, (((0,), (0,)), ((), ())), preferred_element_type=F32)


def legendre_kernel(
    pair, members, degrees, waves, x_ref, y_ref, leg_ref, factor_ref, quad_ref, out_ref, x_wide, y_wide
):
    step = pl.program_id(0)
    x_wide[...] = x_ref[...].astype(F32)
    y_wide[...] = y_ref[...].astype(F32)
    lat_count, _, _, _, rows, lanes = out_ref.shape
    for k in range(pair):
        m = waves[step * pair + k]
        degree = lax.broadcasted_iota(jnp.int32, leg_ref.shape[1:], 0)
        living = (degree >= m) & (m < WAVES)
        basis = jnp.where(living, leg_ref[k].astype(F32), 0.0).astype(BF16)
        for is_cot, wide in enumerate((x_wide, y_wide)):
            parts = []
            for e in range(members):
                part = wide[pl.ds(k * degrees * members + e, degrees, stride=members), :]
                if is_cot:
                    part = TIME_STEP * part * factor_ref[...]
                parts.append(part.astype(BF16))
            result = dot_rows(basis, jnp.concatenate(parts, axis=1))
            if is_cot:
                result = result * quad_ref[...]
            result = result.astype(BF16)
            for e in range(members):
                out_ref[:, e, is_cot, k] = result[:, e * lanes : (e + 1) * lanes].reshape(
                    lat_count, rows, lanes
                )


def legendre(waves, spec, cot, legendre_table, chunk, chunks, lat_count, factor, quad):
    slots, degrees, nlat = legendre_table.shape
    lanes = spec.shape[1]
    members = spec.shape[0] // (slots * degrees)
    pair = 8 if slots % 8 == 0 else 2
    span = nlat // chunks
    rows = span // lat_count
    block = pair * degrees * members
    packed = pl.BlockSpec((block, lanes), lambda i, w: (i, 0))
    return pl.pallas_call(
        functools.partial(legendre_kernel, pair, members, degrees),
        out_shape=jax.ShapeDtypeStruct((lat_count, members, 2, slots, rows, lanes), BF16),
        grid_spec=pltpu.PrefetchScalarGridSpec(
            num_scalar_prefetch=1,
            grid=(slots // pair,),
            in_specs=[
                packed,
                packed,
                pl.BlockSpec((pair, degrees, span), lambda i, w: (i, 0, chunk)),
                pl.BlockSpec((degrees, 1), lambda i, w: (0, 0)),
                pl.BlockSpec((span, 1), lambda i, w: (chunk, 0)),
            ],
            out_specs=pl.BlockSpec(
                (lat_count, members, 2, pair, rows, lanes), lambda i, w: (0, 0, 0, i, 0, 0)
            ),
            scratch_shapes=[pltpu.VMEM((block, lanes), F32)] * 2,
        ),
        compiler_params=pltpu.CompilerParams(
            dimension_semantics=("arbitrary",), vmem_limit_bytes=60 << 20
        ),
        cost_estimate=pl.CostEstimate(
            flops=4 * slots * degrees * span * members * lanes,
            bytes_accessed=4 * spec.size + 2 * slots * span * (degrees + 2 * members * lanes),
            transcendentals=0,
        ),
        name="legendre",
    )(waves, spec, cot, legendre_table, factor, quad)


def inverse_kernel(pair, members, degrees, counts, waves, cot_ref, leg_ref, factor_ref, *rest):
    *backs, out_ref, wide = rest
    step = pl.program_id(0)
    wide[...] = cot_ref[...].astype(F32)
    lanes = cot_ref.shape[1]
    for k in range(pair):
        m = waves[step * pair + k]
        degree = lax.broadcasted_iota(jnp.int32, leg_ref.shape[1:], 0)
        basis = jnp.where((degree >= m) & (m < WAVES), leg_ref[k].astype(F32), 0.0).astype(BF16)
        column = lax.broadcasted_iota(jnp.int32, (degrees, 1), 0)
        shrink = jnp.where((column >= m) & (m < WAVES), factor_ref[...], 0.0)
        sides = []
        for e in range(members):
            pieces, rest_backs = [], list(backs)
            for subs in counts:
                joined = [rest_backs.pop(0)[:, e, k].astype(F32) for _ in range(subs)]
                joined = jnp.concatenate(joined, axis=1) if subs > 1 else joined[0]
                pieces.append(joined.reshape(-1, lanes))
            sides.append(jnp.concatenate(pieces, axis=0).astype(BF16))
        result = dot(basis, jnp.concatenate(sides, axis=1))
        for e in range(members):
            where = pl.ds(k * degrees * members + e, degrees, stride=members)
            out_ref[where, :] = wide[where, :] * shrink + result[:, e * lanes : (e + 1) * lanes]


def inverse_legendre(waves, packed, legendre_table, factor, backs, counts):
    slots, degrees, nlat = legendre_table.shape
    lanes = packed.shape[1]
    members = packed.shape[0] // (slots * degrees)
    pair = 8 if slots % 8 == 0 else 2
    block = pair * degrees * members
    return pl.pallas_call(
        functools.partial(inverse_kernel, pair, members, degrees, counts),
        out_shape=jax.ShapeDtypeStruct(packed.shape, F32),
        grid_spec=pltpu.PrefetchScalarGridSpec(
            num_scalar_prefetch=1,
            grid=(slots // pair,),
            in_specs=[
                pl.BlockSpec((block, lanes), lambda i, w: (i, 0)),
                pl.BlockSpec((pair, degrees, nlat), lambda i, w: (i, 0, 0)),
                pl.BlockSpec((degrees, 1), lambda i, w: (0, 0)),
            ]
            + [
                pl.BlockSpec(b.shape[:2] + (pair,) + b.shape[3:], lambda i, w: (0, 0, i, 0, 0))
                for b in backs
            ],
            out_specs=pl.BlockSpec((block, lanes), lambda i, w: (i, 0)),
            scratch_shapes=[pltpu.VMEM((block, lanes), F32)],
        ),
        compiler_params=pltpu.CompilerParams(
            dimension_semantics=("arbitrary",), vmem_limit_bytes=60 << 20
        ),
        cost_estimate=pl.CostEstimate(
            flops=2 * slots * degrees * nlat * members * lanes,
            bytes_accessed=6 * packed.size + 2 * slots * nlat * (degrees + members * lanes),
            transcendentals=0,
        ),
        name="inverse_legendre",
    )(waves, packed, legendre_table, factor, *backs)


def sigmoid(z):
    return 0.5 + 0.5 * jnp.tanh(0.5 * z)


def column_kernel(
    rows,
    block,
    chained,
    state_ref,
    cot_ref,
    table_ref,
    back_table_ref,
    split_ref,
    merge_ref,
    gain_ref,
    w_in_ref,
    b_in_ref,
    w_mid_ref,
    b_mid_ref,
    w_in_t_ref,
    w_mid_t_ref,
    w_out_t_ref,
    *rest,
):
    if chained:
        before_ref, *rest = rest
    out_ref, grad_ref, state_wide, cot_wide, out_wide, state_mat, cot_mat, back_acc = rest
    row, part = pl.program_id(0), pl.program_id(1)
    last_part = pl.num_programs(1) - 1
    lat_count, groups, slots_here, _, lanes = state_ref.shape
    slots = lat_count * slots_here
    hidden = w_in_ref.shape[1]
    channels = w_in_ref.shape[0]

    @pl.when((row == 0) & (part == 0))
    def _():
        grad_ref[...] = before_ref[...] if chained else jnp.zeros_like(grad_ref)

        @pl.loop(0, lat_count)
        def _(i):
            size = slots_here * rows
            for j in range(groups):
                where = pl.ds(pl.multiple_of(i * size, 8), size)
                state_wide[j, where, :] = state_ref[i, j].astype(F32).reshape(size, lanes)
                cot_wide[j, where, :] = cot_ref[i, j].astype(F32).reshape(size, lanes)

    @pl.when(part == 0)
    def _():
        for wide, mat in ((state_wide, state_mat), (cot_wide, cot_mat)):
            for q in range(groups // 2):
                both = jnp.concatenate(
                    [wide[2 * q + j, pl.ds(row, slots, stride=rows), :].astype(BF16) for j in (0, 1)],
                    axis=1,
                )
                apart = dot(both, split_ref[...]).astype(BF16)
                for p in (0, 1):
                    mat[p * slots : (p + 1) * slots, q * lanes : (q + 1) * lanes] = apart[
                        :, p * lanes : (p + 1) * lanes
                    ]

    table = table_ref[pl.ds(pl.multiple_of(part * block, block), block), :]
    values = dot(table, state_mat[...]).astype(BF16).astype(F32)
    cot = dot(table, cot_mat[...]).astype(BF16)
    gain = gain_ref[...]
    inverse = lax.rsqrt(jnp.mean(values * values, axis=1, keepdims=True) + NORM_EPS)
    unit = values * inverse
    normed = (unit * gain).astype(BF16)
    pre_one = dot(normed, w_in_ref[...]) + b_in_ref[...]
    sig_one = sigmoid(pre_one)
    soft_one = pre_one * sig_one
    slope_one = sig_one + soft_one * (1.0 - sig_one)
    act_one = soft_one.astype(BF16)
    pre_two = dot(act_one, w_mid_ref[...]) + b_mid_ref[...]
    sig_two = sigmoid(pre_two)
    soft_two = pre_two * sig_two
    slope_two = sig_two + soft_two * (1.0 - sig_two)
    act_two = soft_two.astype(BF16)
    delta_two = (dot(cot, w_out_t_ref[...]) * slope_two).astype(BF16)
    delta_one = (dot(delta_two, w_mid_t_ref[...]) * slope_one).astype(BF16)
    back_norm = dot(delta_one, w_in_t_ref[...])
    grad_ref[:channels, :] += dot_rows(normed, delta_one)
    grad_ref[channels : channels + hidden, :] += dot_rows(act_one, delta_two)
    base = channels + hidden
    grad_ref[base : base + channels, :] += dot_rows(cot, act_two)
    base += channels
    grad_ref[base : base + 1, :] += jnp.sum(delta_one.astype(F32), axis=0, keepdims=True)
    grad_ref[base + 1 : base + 2, :] += jnp.sum(delta_two.astype(F32), axis=0, keepdims=True)
    grad_ref[base + 2 : base + 3, :channels] += jnp.sum(back_norm * unit, axis=0, keepdims=True)
    scaled = back_norm * gain
    mean = jnp.mean(scaled * values, axis=1, keepdims=True)
    grad_columns = (inverse * scaled - values * (inverse * inverse * inverse) * mean).astype(BF16)
    back = dot(back_table_ref[:, pl.ds(pl.multiple_of(part * block, block), block)], grad_columns)

    @pl.when(part == 0)
    def _():
        back_acc[...] = back

    @pl.when(part > 0)
    def _():
        back_acc[...] += back

    @pl.when(part == last_part)
    def _():
        for q in range(groups // 2):
            apart = jnp.concatenate(
                [
                    back_acc[p * slots : (p + 1) * slots, q * lanes : (q + 1) * lanes].astype(BF16)
                    for p in (0, 1)
                ],
                axis=1,
            )
            both = dot(apart, merge_ref[...])
            for j in (0, 1):
                out_wide[2 * q + j, pl.ds(row, slots, stride=rows), :] = both[
                    :, j * lanes : (j + 1) * lanes
                ]

    @pl.when((row == rows - 1) & (part == last_part))
    def _():
        @pl.loop(0, lat_count)
        def _(i):
            size = slots_here * rows
            for j in range(groups):
                where = pl.ds(pl.multiple_of(i * size, 8), size)
                out_ref[i, j] = out_wide[j, where, :].astype(BF16).reshape(slots_here, rows, lanes)


def column_grads(pair, sub, rows, table, back_table, split, merge, gain, weights, before):
    lat_count, groups, _, slots_here, _, lanes = pair.shape
    slots = lat_count * slots_here
    weight_in, bias_in, weight_mid, bias_mid, weight_out = weights
    channels, hidden = weight_in.shape
    block = NLON
    grad_rows = -(-(2 * channels + hidden + 3) // 64) * 64
    operands = [
        table,
        back_table,
        split,
        merge,
        gain,
        weight_in,
        bias_in[None, :],
        weight_mid,
        bias_mid[None, :],
        weight_in.T,
        weight_mid.T,
        weight_out.T,
    ]
    if before is not None:
        operands.append(before)

    def whole(shape):
        return pl.BlockSpec(shape, lambda i, j: (0,) * len(shape), pipeline_mode=pl.Buffered(1))

    def source(which):
        return pl.BlockSpec(
            (lat_count, groups, None, slots_here, rows, lanes),
            lambda i, j: (0, 0, which, 0, sub, 0),
            pipeline_mode=pl.Buffered(1),
        )

    out_shapes = (
        jax.ShapeDtypeStruct((lat_count, groups, slots_here, rows, lanes), BF16),
        jax.ShapeDtypeStruct((grad_rows, hidden), F32),
    )
    wide = pltpu.VMEM((groups, slots * rows, lanes), F32)
    mat = pltpu.VMEM((2 * slots, channels), BF16)
    per_column = channels * hidden * 6 + hidden * hidden * 3 + 6 * slots * channels
    return pl.pallas_call(
        functools.partial(column_kernel, rows, block, before is not None),
        out_shape=out_shapes,
        grid=(rows, NLON // block),
        in_specs=[source(0), source(1)] + [whole(o.shape) for o in operands],
        out_specs=tuple(whole(o.shape) for o in out_shapes),
        scratch_shapes=[wide, wide, wide, mat, mat, pltpu.VMEM((2 * slots, channels), F32)],
        compiler_params=pltpu.CompilerParams(
            dimension_semantics=("arbitrary", "arbitrary"), vmem_limit_bytes=60 << 20
        ),
        cost_estimate=pl.CostEstimate(
            flops=2 * rows * NLON * per_column,
            bytes_accessed=6 * slots * rows * groups * lanes + 8 * grad_rows * hidden,
            transcendentals=2 * rows * NLON * hidden,
        ),
        name="columns",
    )(pair, pair, *operands)


def swap(x, axis, bits):
    return lax.ppermute(x, axis, [(i, i ^ bits) for i in range(lax.axis_size(axis))])


def reduce_grads(total):
    top = lax.axis_size("lat") // 4
    steps = []
    for axis, limit in (("lev", lax.axis_size("lev")), ("lat", top)):
        bit = 1
        while bit < limit:
            steps.append((axis, bit))
            bit *= 2
    for axis, bit in steps:
        size = total.shape[0] // 2
        side = (lax.axis_index(axis) // bit) % 2
        sent = lax.dynamic_slice_in_dim(total, (1 - side) * size, size).astype(BF16)
        kept = lax.dynamic_slice_in_dim(total, side * size, size)
        total = kept + swap(sent, axis, bit).astype(F32)
    part = total.astype(BF16)
    for k in (1, 2):
        part = (part.astype(F32) + swap(part, "lat", k * top).astype(F32)).astype(BF16)
    for axis, bit in reversed(steps):
        side = (lax.axis_index(axis) // bit) % 2
        other = swap(part, axis, bit)
        first, second = jnp.where(side == 0, part, other), jnp.where(side == 0, other, part)
        part = jnp.concatenate([first, second], axis=0)
    return part.astype(F32)


def step(
    spec_in,
    cotangent,
    legendre_table,
    quad_weights,
    wave_order,
    norm_gain,
    weight_in,
    bias_in,
    weight_mid,
    bias_mid,
    weight_out,
):
    axes = ("lat", "lev")
    slots_here, degrees, members, lanes = spec_in.shape
    nlat = legendre_table.shape[2]
    lat_count = lax.axis_size("lat")
    lev_count = lax.axis_size("lev")
    assert members == lev_count
    chunks = 2 if nlat // lat_count >= 16 else 1
    own_waves = lax.dynamic_slice_in_dim(wave_order, lax.axis_index("lat") * slots_here, slots_here)
    factor = shrink_factor(degrees)
    quad = quad_weights[:, None]
    spec_rows = spec_in.reshape(slots_here * degrees * members, lanes)
    cot_rows = cotangent.reshape(slots_here * degrees * members, lanes)
    count = lat_count * lev_count

    def exchange(x):
        shape = x.shape
        x = x.reshape((count,) + shape[2:])
        x = lax.all_to_all(x, axes, split_axis=0, concat_axis=0, tiled=True)
        return x.reshape(shape)

    table = fourier_table(wave_order)
    split = split_parts(lanes)
    rows = nlat // chunks // lat_count
    subs = rows // 8
    received = []
    for k in range(chunks):
        pair = legendre(
            own_waves, spec_rows, cot_rows, legendre_table, k, chunks, lat_count, factor, quad
        )
        if received:
            pair, received[-1] = lax.optimization_barrier((pair, received[-1]))
        received.append(exchange(pair))
    weights = (weight_in, bias_in, weight_mid, bias_mid, weight_out)
    gain = norm_gain[None, :]
    counts = (1,) * (chunks - 1) + (subs,)
    backs, total = [], None
    for k, pair in enumerate(received):
        for sub in range(counts[k]):
            back, total = column_grads(
                pair, sub, rows // counts[k], table.T, table, split, split.T, gain, weights, total
            )
            backs.append(exchange(back))
    summed = reduce_grads(total)
    channels, hidden = weight_in.shape
    summed = summed * float(members * nlat * NLON) ** (-0.5)
    base = 2 * channels + hidden
    grad_w_in = summed[:channels]
    grad_w_mid = summed[channels : channels + hidden]
    grad_w_out = summed[channels + hidden : base].T
    grad_spec = inverse_legendre(own_waves, cot_rows, legendre_table, factor, backs, counts)
    return (
        grad_spec.reshape(spec_in.shape),
        summed[base + 2, :channels],
        grad_w_in,
        summed[base],
        grad_w_mid,
        summed[base + 1],
        grad_w_out,
    )


def solution(mesh):
    placed = (
        P("lat", None, None, "lev"),
        P("lat", None, None, "lev"),
        P("lat", None, None),
    ) + (P(),) * 8
    return jax.shard_map(
        step,
        mesh=mesh,
        in_specs=placed,
        out_specs=(P("lat", None, None, "lev"),) + (P(),) * 6,
        check_vma=False,
    )
```

```python
import functools
import math

import jax
import jax.numpy as jnp
from jax import lax
from jax.experimental import pallas as pl
from jax.experimental.pallas import tpu as pltpu
from jax.sharding import PartitionSpec as P

WAVES = 171
TIME_STEP = 0.5
NORM_EPS = 1e-06
NLON = 512
F32 = jnp.float32
BF16 = jnp.bfloat16


def fourier_table(waves_all):
    longitude = jnp.arange(NLON, dtype=jnp.int32)
    phase_steps = waves_all[:, None] * longitude[None, :] % NLON
    angles = phase_steps.astype(F32) * (2.0 * math.pi / NLON)
    weight_scale = jnp.where(waves_all < WAVES, math.sqrt(2.0 / NLON), 0.0).astype(F32)[:, None]
    return jnp.concatenate(
        [jnp.cos(angles) * weight_scale, -jnp.sin(angles) * weight_scale], axis=0
    ).astype(BF16)


def shrink_factor(degree_count):
    degree = jnp.arange(degree_count, dtype=jnp.int32)
    ratio = (degree * (degree + 1)).astype(F32) / float(WAVES * (WAVES - 1))
    return (1.0 / (1.0 + ratio * ratio))[:, None]


def split_parts(half):
    width = 2 * half
    src = lax.broadcasted_iota(jnp.int32, (width, width), 0)
    dst = lax.broadcasted_iota(jnp.int32, (width, width), 1)
    group, inner = src // half, src % half
    target = (inner % 2) * half + group * (half // 2) + inner // 2
    return (target == dst).astype(BF16)


def dot(left, right):
    return jnp.dot(left, right, preferred_element_type=F32)


def dot_rows(left, right):
    return lax.dot_general(left, right, (((0,), (0,)), ((), ())), preferred_element_type=F32)


def legendre_kernel(
    pair,
    members,
    degrees,
    swapped,
    waves,
    x_ref,
    y_ref,
    leg_ref,
    factor_ref,
    quad_ref,
    out_ref,
    x_wide,
    y_wide,
    *leg_wide,
):
    step = pl.program_id(0)
    x_wide[...] = x_ref[...].astype(F32)
    y_wide[...] = y_ref[...].astype(F32)
    lat_count, _, _, _, rows, lanes = out_ref.shape
    span = leg_ref.shape[2]
    if swapped:
        (leg_wide,) = leg_wide
        leg_wide[...] = leg_ref[...].astype(F32).reshape(degrees * pair, span)
    for k in range(pair):
        m = waves[step * pair + k]
        degree = lax.broadcasted_iota(jnp.int32, (degrees, span), 0)
        living = (degree >= m) & (m < WAVES)
        if swapped:
            values = leg_wide[pl.ds(k, degrees, stride=pair), :]
        else:
            values = leg_ref[k].astype(F32)
        basis = jnp.where(living, values, 0.0).astype(BF16)
        for is_cot, wide in enumerate((x_wide, y_wide)):
            parts = []
            for e in range(members):
                part = wide[pl.ds(k * degrees * members + e, degrees, stride=members), :]
                if is_cot:
                    part = TIME_STEP * part * factor_ref[...]
                parts.append(part.astype(BF16))
            result = dot_rows(basis, jnp.concatenate(parts, axis=1))
            if is_cot:
                result = result * quad_ref[...]
            result = result.astype(BF16)
            for e in range(members):
                out_ref[:, e, is_cot, k] = result[:, e * lanes : (e + 1) * lanes].reshape(
                    lat_count, rows, lanes
                )


def legendre(waves, spec, cot, legendre_table, chunk, chunks, lat_count, factor, quad):
    slots, degrees, nlat = legendre_table.shape
    lanes = spec.shape[1]
    members = spec.shape[0] // (slots * degrees)
    pair = 8 if slots % 8 == 0 else 2
    span = nlat // chunks
    rows = span // lat_count
    block = pair * degrees * members
    packed = pl.BlockSpec((block, lanes), lambda i, w: (i, 0))
    swapped = chunk == 0 and pair == 8 and span == 128
    scratch = [pltpu.VMEM((block, lanes), F32)] * 2
    table_spec = pl.BlockSpec((pair, degrees, span), lambda i, w: (i, 0, chunk))
    if swapped:
        legendre_table = jnp.transpose(legendre_table, (1, 0, 2))
        table_spec = pl.BlockSpec((degrees, pair, span), lambda i, w: (0, i, chunk))
        scratch.append(pltpu.VMEM((degrees * pair, span), F32))
    return pl.pallas_call(
        functools.partial(legendre_kernel, pair, members, degrees, swapped),
        out_shape=jax.ShapeDtypeStruct((lat_count, members, 2, slots, rows, lanes), BF16),
        grid_spec=pltpu.PrefetchScalarGridSpec(
            num_scalar_prefetch=1,
            grid=(slots // pair,),
            in_specs=[
                packed,
                packed,
                table_spec,
                pl.BlockSpec((degrees, 1), lambda i, w: (0, 0)),
                pl.BlockSpec((span, 1), lambda i, w: (chunk, 0)),
            ],
            out_specs=pl.BlockSpec(
                (lat_count, members, 2, pair, rows, lanes), lambda i, w: (0, 0, 0, i, 0, 0)
            ),
            scratch_shapes=scratch,
        ),
        compiler_params=pltpu.CompilerParams(
            dimension_semantics=("arbitrary",), vmem_limit_bytes=60 << 20
        ),
        cost_estimate=pl.CostEstimate(
            flops=4 * slots * degrees * span * members * lanes,
            bytes_accessed=4 * spec.size + 2 * slots * span * (degrees + 2 * members * lanes),
            transcendentals=0,
        ),
        name="legendre",
    )(waves, spec, cot, legendre_table, factor, quad)


def inverse_kernel(pair, members, degrees, counts, waves, cot_ref, leg_ref, factor_ref, *rest):
    *backs, out_ref, wide = rest
    step = pl.program_id(0)
    wide[...] = cot_ref[...].astype(F32)
    lanes = cot_ref.shape[1]
    for k in range(pair):
        m = waves[step * pair + k]
        degree = lax.broadcasted_iota(jnp.int32, leg_ref.shape[1:], 0)
        basis = jnp.where((degree >= m) & (m < WAVES), leg_ref[k].astype(F32), 0.0).astype(BF16)
        column = lax.broadcasted_iota(jnp.int32, (degrees, 1), 0)
        shrink = jnp.where((column >= m) & (m < WAVES), factor_ref[...], 0.0)
        sides = []
        for e in range(members):
            pieces, rest_backs = [], list(backs)
            for subs in counts:
                joined = [rest_backs.pop(0)[:, e, k].astype(F32) for _ in range(subs)]
                joined = jnp.concatenate(joined, axis=1) if subs > 1 else joined[0]
                pieces.append(joined.reshape(-1, lanes))
            sides.append(jnp.concatenate(pieces, axis=0).astype(BF16))
        result = dot(basis, jnp.concatenate(sides, axis=1))
        for e in range(members):
            where = pl.ds(k * degrees * members + e, degrees, stride=members)
            out_ref[where, :] = wide[where, :] * shrink + result[:, e * lanes : (e + 1) * lanes]


def inverse_legendre(waves, packed, legendre_table, factor, backs, counts):
    slots, degrees, nlat = legendre_table.shape
    lanes = packed.shape[1]
    members = packed.shape[0] // (slots * degrees)
    pair = 8 if slots % 8 == 0 else 2
    block = pair * degrees * members
    return pl.pallas_call(
        functools.partial(inverse_kernel, pair, members, degrees, counts),
        out_shape=jax.ShapeDtypeStruct(packed.shape, F32),
        grid_spec=pltpu.PrefetchScalarGridSpec(
            num_scalar_prefetch=1,
            grid=(slots // pair,),
            in_specs=[
                pl.BlockSpec((block, lanes), lambda i, w: (i, 0)),
                pl.BlockSpec((pair, degrees, nlat), lambda i, w: (i, 0, 0)),
                pl.BlockSpec((degrees, 1), lambda i, w: (0, 0)),
            ]
            + [
                pl.BlockSpec(b.shape[:2] + (pair,) + b.shape[3:], lambda i, w: (0, 0, i, 0, 0))
                for b in backs
            ],
            out_specs=pl.BlockSpec((block, lanes), lambda i, w: (i, 0)),
            scratch_shapes=[pltpu.VMEM((block, lanes), F32)],
        ),
        compiler_params=pltpu.CompilerParams(
            dimension_semantics=("arbitrary",), vmem_limit_bytes=60 << 20
        ),
        cost_estimate=pl.CostEstimate(
            flops=2 * slots * degrees * nlat * members * lanes,
            bytes_accessed=6 * packed.size + 2 * slots * nlat * (degrees + members * lanes),
            transcendentals=0,
        ),
        name="inverse_legendre",
    )(waves, packed, legendre_table, factor, *backs)


def sigmoid(z):
    return 0.5 + 0.5 * jnp.tanh(0.5 * z)


def column_kernel(
    rows,
    block,
    chained,
    state_ref,
    cot_ref,
    table_ref,
    back_table_ref,
    split_ref,
    merge_ref,
    gain_ref,
    w_in_ref,
    b_in_ref,
    w_mid_ref,
    b_mid_ref,
    w_in_t_ref,
    w_mid_t_ref,
    w_out_t_ref,
    *rest,
):
    if chained:
        before_ref, *rest = rest
    out_ref, grad_ref, state_wide, cot_wide, out_wide, state_mat, cot_mat, back_acc = rest
    row, part = pl.program_id(0), pl.program_id(1)
    last_part = pl.num_programs(1) - 1
    lat_count, groups, slots_here, _, lanes = state_ref.shape
    slots = lat_count * slots_here
    hidden = w_in_ref.shape[1]
    channels = w_in_ref.shape[0]

    @pl.when((row == 0) & (part == 0))
    def _():
        grad_ref[...] = before_ref[...] if chained else jnp.zeros_like(grad_ref)

        @pl.loop(0, lat_count)
        def _(i):
            size = slots_here * rows
            for j in range(groups):
                where = pl.ds(pl.multiple_of(i * size, 8), size)
                state_wide[j, where, :] = state_ref[i, j].astype(F32).reshape(size, lanes)
                cot_wide[j, where, :] = cot_ref[i, j].astype(F32).reshape(size, lanes)

    @pl.when(part == 0)
    def _():
        for wide, mat in ((state_wide, state_mat), (cot_wide, cot_mat)):
            for q in range(groups // 2):
                both = jnp.concatenate(
                    [wide[2 * q + j, pl.ds(row, slots, stride=rows), :].astype(BF16) for j in (0, 1)],
                    axis=1,
                )
                apart = dot(both, split_ref[...]).astype(BF16)
                for p in (0, 1):
                    mat[p * slots : (p + 1) * slots, q * lanes : (q + 1) * lanes] = apart[
                        :, p * lanes : (p + 1) * lanes
                    ]

    table = table_ref[pl.ds(pl.multiple_of(part * block, block), block), :]
    values = dot(table, state_mat[...]).astype(BF16).astype(F32)
    cot = dot(table, cot_mat[...]).astype(BF16)
    gain = gain_ref[...]
    inverse = lax.rsqrt(jnp.mean(values * values, axis=1, keepdims=True) + NORM_EPS)
    unit = values * inverse
    normed = (unit * gain).astype(BF16)
    pre_one = dot(normed, w_in_ref[...]) + b_in_ref[...]
    sig_one = sigmoid(pre_one)
    soft_one = pre_one * sig_one
    slope_one = sig_one + soft_one * (1.0 - sig_one)
    act_one = soft_one.astype(BF16)
    pre_two = dot(act_one, w_mid_ref[...]) + b_mid_ref[...]
    sig_two = sigmoid(pre_two)
    soft_two = pre_two * sig_two
    slope_two = sig_two + soft_two * (1.0 - sig_two)
    act_two = soft_two.astype(BF16)
    delta_two = (dot(cot, w_out_t_ref[...]) * slope_two).astype(BF16)
    delta_one = (dot(delta_two, w_mid_t_ref[...]) * slope_one).astype(BF16)
    back_norm = dot(delta_one, w_in_t_ref[...])
    grad_ref[:channels, :] += dot_rows(normed, delta_one)
    grad_ref[channels : channels + hidden, :] += dot_rows(act_one, delta_two)
    base = channels + hidden
    grad_ref[base : base + channels, :] += dot_rows(cot, act_two)
    base += channels
    grad_ref[base : base + 1, :] += jnp.sum(delta_one.astype(F32), axis=0, keepdims=True)
    grad_ref[base + 1 : base + 2, :] += jnp.sum(delta_two.astype(F32), axis=0, keepdims=True)
    grad_ref[base + 2 : base + 3, :channels] += jnp.sum(back_norm * unit, axis=0, keepdims=True)
    scaled = back_norm * gain
    mean = jnp.mean(scaled * values, axis=1, keepdims=True)
    grad_columns = (inverse * scaled - values * (inverse * inverse * inverse) * mean).astype(BF16)
    back = dot(back_table_ref[:, pl.ds(pl.multiple_of(part * block, block), block)], grad_columns)

    @pl.when(part == 0)
    def _():
        back_acc[...] = back

    @pl.when(part > 0)
    def _():
        back_acc[...] += back

    @pl.when(part == last_part)
    def _():
        for q in range(groups // 2):
            apart = jnp.concatenate(
                [
                    back_acc[p * slots : (p + 1) * slots, q * lanes : (q + 1) * lanes].astype(BF16)
                    for p in (0, 1)
                ],
                axis=1,
            )
            both = dot(apart, merge_ref[...])
            for j in (0, 1):
                out_wide[2 * q + j, pl.ds(row, slots, stride=rows), :] = both[
                    :, j * lanes : (j + 1) * lanes
                ]

    @pl.when((row == rows - 1) & (part == last_part))
    def _():
        @pl.loop(0, lat_count)
        def _(i):
            size = slots_here * rows
            for j in range(groups):
                where = pl.ds(pl.multiple_of(i * size, 8), size)
                out_ref[i, j] = out_wide[j, where, :].astype(BF16).reshape(slots_here, rows, lanes)


def column_grads(pair, sub, rows, table, back_table, split, merge, gain, weights, before):
    lat_count, groups, _, slots_here, _, lanes = pair.shape
    slots = lat_count * slots_here
    weight_in, bias_in, weight_mid, bias_mid, weight_out = weights
    channels, hidden = weight_in.shape
    block = NLON
    grad_rows = -(-(2 * channels + hidden + 3) // 64) * 64
    operands = [
        table,
        back_table,
        split,
        merge,
        gain,
        weight_in,
        bias_in[None, :],
        weight_mid,
        bias_mid[None, :],
        weight_in.T,
        weight_mid.T,
        weight_out.T,
    ]
    if before is not None:
        operands.append(before)

    def whole(shape):
        return pl.BlockSpec(shape, lambda i, j: (0,) * len(shape), pipeline_mode=pl.Buffered(1))

    def source(which):
        return pl.BlockSpec(
            (lat_count, groups, None, slots_here, rows, lanes),
            lambda i, j: (0, 0, which, 0, sub, 0),
            pipeline_mode=pl.Buffered(1),
        )

    out_shapes = (
        jax.ShapeDtypeStruct((lat_count, groups, slots_here, rows, lanes), BF16),
        jax.ShapeDtypeStruct((grad_rows, hidden), F32),
    )
    wide = pltpu.VMEM((groups, slots * rows, lanes), F32)
    mat = pltpu.VMEM((2 * slots, channels), BF16)
    per_column = channels * hidden * 6 + hidden * hidden * 3 + 6 * slots * channels
    return pl.pallas_call(
        functools.partial(column_kernel, rows, block, before is not None),
        out_shape=out_shapes,
        grid=(rows, NLON // block),
        in_specs=[source(0), source(1)] + [whole(o.shape) for o in operands],
        out_specs=tuple(whole(o.shape) for o in out_shapes),
        scratch_shapes=[wide, wide, wide, mat, mat, pltpu.VMEM((2 * slots, channels), F32)],
        compiler_params=pltpu.CompilerParams(
            dimension_semantics=("arbitrary", "arbitrary"), vmem_limit_bytes=60 << 20
        ),
        cost_estimate=pl.CostEstimate(
            flops=2 * rows * NLON * per_column,
            bytes_accessed=6 * slots * rows * groups * lanes + 8 * grad_rows * hidden,
            transcendentals=2 * rows * NLON * hidden,
        ),
        name="columns",
    )(pair, pair, *operands)


def swap(x, axis, bits):
    return lax.ppermute(x, axis, [(i, i ^ bits) for i in range(lax.axis_size(axis))])


def reduce_grads(total):
    top = lax.axis_size("lat") // 4
    steps = []
    for axis, limit in (("lev", lax.axis_size("lev")), ("lat", top)):
        bit = 1
        while bit < limit:
            steps.append((axis, bit))
            bit *= 2
    for axis, bit in steps:
        size = total.shape[0] // 2
        side = (lax.axis_index(axis) // bit) % 2
        sent = lax.dynamic_slice_in_dim(total, (1 - side) * size, size).astype(BF16)
        kept = lax.dynamic_slice_in_dim(total, side * size, size)
        total = kept + swap(sent, axis, bit).astype(F32)
    part = total.astype(BF16)
    for k in (1, 2):
        part = (part.astype(F32) + swap(part, "lat", k * top).astype(F32)).astype(BF16)
    for axis, bit in reversed(steps):
        side = (lax.axis_index(axis) // bit) % 2
        other = swap(part, axis, bit)
        first, second = jnp.where(side == 0, part, other), jnp.where(side == 0, other, part)
        part = jnp.concatenate([first, second], axis=0)
    return part.astype(F32)


def step(
    spec_in,
    cotangent,
    legendre_table,
    quad_weights,
    wave_order,
    norm_gain,
    weight_in,
    bias_in,
    weight_mid,
    bias_mid,
    weight_out,
):
    axes = ("lat", "lev")
    slots_here, degrees, members, lanes = spec_in.shape
    nlat = legendre_table.shape[2]
    lat_count = lax.axis_size("lat")
    lev_count = lax.axis_size("lev")
    assert members == lev_count
    chunks = 2 if nlat // lat_count >= 16 else 1
    own_waves = lax.dynamic_slice_in_dim(wave_order, lax.axis_index("lat") * slots_here, slots_here)
    factor = shrink_factor(degrees)
    quad = quad_weights[:, None]
    spec_rows = spec_in.reshape(slots_here * degrees * members, lanes)
    cot_rows = cotangent.reshape(slots_here * degrees * members, lanes)
    count = lat_count * lev_count

    def exchange(x):
        shape = x.shape
        x = x.reshape((count,) + shape[2:])
        x = lax.all_to_all(x, axes, split_axis=0, concat_axis=0, tiled=True)
        return x.reshape(shape)

    table = fourier_table(wave_order)
    split = split_parts(lanes)
    rows = nlat // chunks // lat_count
    subs = rows // 8
    received = []
    for k in range(chunks):
        pair = legendre(
            own_waves, spec_rows, cot_rows, legendre_table, k, chunks, lat_count, factor, quad
        )
        if received:
            pair, received[-1] = lax.optimization_barrier((pair, received[-1]))
        received.append(exchange(pair))
    weights = (weight_in, bias_in, weight_mid, bias_mid, weight_out)
    gain = norm_gain[None, :]
    counts = (1,) * (chunks - 1) + (subs,)
    backs, total = [], None
    for k, pair in enumerate(received):
        for sub in range(counts[k]):
            back, total = column_grads(
                pair, sub, rows // counts[k], table.T, table, split, split.T, gain, weights, total
            )
            backs.append(exchange(back))
    summed = reduce_grads(total)
    channels, hidden = weight_in.shape
    summed = summed * float(members * nlat * NLON) ** (-0.5)
    base = 2 * channels + hidden
    grad_w_in = summed[:channels]
    grad_w_mid = summed[channels : channels + hidden]
    grad_w_out = summed[channels + hidden : base].T
    grad_spec = inverse_legendre(own_waves, cot_rows, legendre_table, factor, backs, counts)
    return (
        grad_spec.reshape(spec_in.shape),
        summed[base + 2, :channels],
        grad_w_in,
        summed[base],
        grad_w_mid,
        summed[base + 1],
        grad_w_out,
    )


def solution(mesh):
    placed = (
        P("lat", None, None, "lev"),
        P("lat", None, None, "lev"),
        P("lat", None, None),
    ) + (P(),) * 8
    return jax.shard_map(
        step,
        mesh=mesh,
        in_specs=placed,
        out_specs=(P("lat", None, None, "lev"),) + (P(),) * 6,
        check_vma=False,
    )
```
